32 devices in a mesh: group: 2 (over x), src: 16 (over z, y, core).
Axes of the slice: x: 2, y: 2, z: 4, core: 2. Of those that a mesh axis runs over, the one named last changes fastest.
Arguments:
- positions: float32 [2, 32768], P(None, ('group', 'src')), parts along dimension 1, may hold values from -0.2 to 0.2
- flux: float32 [4, 32768], P(None, ('group', 'src')), parts along dimension 1, may hold values from 0.1 to 2
- cluster: int32 [32768], P(('group', 'src')), parts along dimension 0, may hold values from 0 to 15
- jones: float32 [4, 2, 16, 1024], P(None, None, None, ('group', 'src')), parts along dimension 3, may hold values from -4 to 4
- station_uvw: float32 [3, 1024], P(None, ('group', 'src')), parts along dimension 1, may hold values from -600 to 600
- channels: int32 [8], P('group'), parts along dimension 0, may hold values from 0 to 383
- tile_map: int32 [32, 2], P('group'), parts along dimension 0, may hold values from 0 to 15, as said below
Outputs:
- visibilities: float32 [32, 4, 2, 1024], P(('group', 'src')), parts along dimension 0
The draws below stay inside these ranges and needn't reach their ends.
There are 2 independent parts, one for each index of `group`. The reference program is written for one: setup_inputs(seed, part) draws one part's arguments, and reference() takes and returns one part's arrays. A program takes and returns all parts, laid end to end along the dimension named above; each array names one. Nothing has to cross between parts.
Inputs may be any that keep to these rules, and one draw needn't show every extreme that they name: `tile_map`: each row is a pair of station tiles (first, second) with first <= second; the 16 pairs are distinct.
All inputs are finite; a program needn't handle non-finite values.
Results may differ from the reference program's by a relative error of at most 0.0038.
Values sent between devices are 32-bit elements; how exact they have to be, the bound alone decides.
A program may use at most 128 MiB of HBM per device.

```python
import math
import jax
import jax.numpy as jnp
import numpy as np
from jax import lax

S = 512
C = 4
K = 16
TS = 32
SOURCES = 16384
BLOCKS = 16


def draw_tile_map(key, part):
    tiles = S // TS
    table = np.array([(first, second) for first in range(tiles) for second in range(first, tiles)], np.int32)
    count = table.shape[0]
    key_one, key_two = jax.random.split(jax.random.fold_in(key, 7))
    scores = jax.random.randint(key_one, (count,), 0, 1 << 20) * 256 + jnp.arange(count, dtype=jnp.int32)
    scores = scores.at[tiles - 1].set(1 << 29)
    order = jnp.argsort(-scores, stable=True)[:BLOCKS]
    shuffle = jax.random.permutation(key_two, BLOCKS)
    chosen = order[shuffle]
    return jnp.asarray(table)[chosen]


def place_ends(values, own_key, smallest, high):
    dims = values.shape
    index_at = [jax.random.randint(jax.random.fold_in(own_key, axis), (), 0, dims[axis]) for axis in range(len(dims))]
    values = values.at[tuple(index_at)].set(smallest)
    longest = dims.index(max(dims))
    index_at[longest] = (index_at[longest] + 1) % dims[longest]
    return values.at[tuple(index_at)].set(high)


def block_levels(own_key, dims, cuts, smallest, high):
    factor_of, own = 1.0, jax.random.fold_in(own_key, 6)
    for dim, parts in cuts:
        steps = jnp.exp(jax.random.uniform(jax.random.fold_in(own, dim), (parts,), jnp.float32, smallest / len(cuts), high / len(cuts)))
        factor_of = factor_of * jnp.repeat(steps, dims[dim] // parts).reshape([-1 if axis == dim else 1 for axis in range(len(dims))])
    return factor_of


def gaussian(rng, extent, spread, limit, cuts=(), held_as=jnp.bfloat16):
    gain = block_levels(rng, extent, cuts, -0.22, 0.18) if cuts else 1.0
    drawn = jax.random.normal(rng, extent, jnp.float32) * spread * gain
    return jnp.minimum(jnp.maximum(drawn, -limit), limit).astype(held_as)


def setup_inputs(seed: int = 0, part: int = 0) -> dict:
    splits = jax.random.split(jax.random.key(seed), 8)
    part_splits = jax.random.split(jax.random.fold_in(splits[7], part), 8)
    return {
        "positions": jnp.clip(jax.random.uniform(part_splits[0], (2, SOURCES), jnp.float32, -0.2, 0.2) * block_levels(part_splits[0], (2, SOURCES), ((1, 16),), -0.4, 0.0), -0.2, 0.2),
        "flux": jnp.clip(jnp.exp(math.log(2.0) - 2.9957323 * jax.random.uniform(part_splits[1], (C, SOURCES), jnp.float32) ** block_levels(part_splits[1], (C, SOURCES), ((1, 16),), -0.2, 0.2)), 0.1, 2.0),
        "cluster": place_ends(jax.random.randint(part_splits[2], (SOURCES,), 0, K), jax.random.fold_in(part_splits[2], 1), 0, K - 1).astype(jnp.int32),
        "jones": gaussian(part_splits[3], (C, 2, K, S), 0.7, 4.0, ((3, 16),), jnp.float32),
        "station_uvw": gaussian(part_splits[4], (3, S), 100.0, 600.0, ((1, 16),), jnp.float32),
        "channels": place_ends(jax.random.randint(part_splits[5], (C,), 0, 384), jax.random.fold_in(part_splits[5], 1), 0, 383).astype(jnp.int32),
        "tile_map": draw_tile_map(jax.random.fold_in(jax.random.fold_in(splits[7], part), 71), part),
    }


def phasors(station_gain, coords_uvw, coords, cluster_val, freq_ratio):
    directions = station_gain.shape[2]
    onehot = (cluster_val[None, :] == jnp.arange(directions, dtype=jnp.float32)[:, None]).astype(jnp.float32)
    gain_re = jnp.einsum('ckp,kn->cpn', station_gain[:, 0], onehot, precision=lax.Precision.HIGHEST)
    gain_im = jnp.einsum('ckp,kn->cpn', station_gain[:, 1], onehot, precision=lax.Precision.HIGHEST)
    l_term = coords[0]
    m_term = coords[1]
    n_term = jnp.sqrt(1.0 - l_term * l_term - m_term * m_term)
    argument = coords_uvw[0][:, None] * l_term[None, :] + coords_uvw[1][:, None] * m_term[None, :] + coords_uvw[2][:, None] * (n_term - 1.0)[None, :]
    phase = (2.0 * math.pi * freq_ratio)[:, None, None] * argument[None]
    cosine = jnp.cos(phase)
    sine = jnp.sin(phase)
    real_part = gain_re * cosine + gain_im * sine
    imag_part = gain_im * cosine - gain_re * sine
    return (real_part, imag_part)

def weighted_side(real_part, imag_part, fluxes, scale):
    weight = fluxes[:, None, :] * scale
    return jnp.stack([real_part * weight, imag_part * weight], 2).astype(jnp.bfloat16)

def plain_side(real_part, imag_part):
    return jnp.stack([real_part, imag_part], 2).astype(jnp.bfloat16)

def reference(positions, flux, cluster, jones, station_uvw, channels, tile_map):
    freq_ratio = 1.0 + 0.002 * channels.astype(jnp.float32)
    scale = 1.0 / math.sqrt(SOURCES)
    width = math.gcd(SOURCES, 4096)
    turns = SOURCES // width
    first_tile = tile_map[:, 0]
    second_tile = tile_map[:, 1]
    tiles = S // TS
    chans = jones.shape[0]

    def accumulate(total, turn):
        begin = (turn * width).astype(jnp.int32)
        coords = lax.dynamic_slice_in_dim(positions, begin, width, 1)
        fluxes = lax.dynamic_slice_in_dim(flux, begin, width, 1)
        cluster_val = lax.dynamic_slice_in_dim(cluster, begin, width, 0).astype(jnp.float32)
        real_part, imag_part = phasors(jones, station_uvw, coords, cluster_val, freq_ratio)
        weighted = weighted_side(real_part, imag_part, fluxes, scale).reshape(chans, tiles, TS, 2, width)
        plain = plain_side(real_part, imag_part).reshape(chans, tiles, TS, 2, width)
        left_sel = jnp.take(weighted, first_tile, axis=1).astype(jnp.float32)
        right_sel = jnp.take(plain, second_tile, axis=1).astype(jnp.float32)
        real_sum = jnp.einsum('cbirx,cbjrx->bcij', left_sel, right_sel)
        imag_sum = jnp.einsum('cbix,cbjx->bcij', left_sel[:, :, :, 1], right_sel[:, :, :, 0]) - jnp.einsum('cbix,cbjx->bcij', left_sel[:, :, :, 0], right_sel[:, :, :, 1])
        return (total + jnp.stack([real_sum, imag_sum], 2), None)
    blocks = tile_map.shape[0]
    start_total = jnp.zeros((blocks, chans, 2, TS, TS), jnp.float32)
    total, unused = lax.scan(accumulate, start_total, jnp.arange(turns, dtype=jnp.int32))
    same_tile = (first_tile == second_tile)[:, None, None, None, None]
    diagonal = (jnp.arange(TS)[:, None] == jnp.arange(TS)[None, :])[None, None, None]
    total = jnp.where(same_tile & diagonal, jnp.float32(0.0), total)
    return total.reshape(blocks, chans, 2, TS * TS)
```

```python
import functools
import math

import jax
import jax.numpy as jnp
from jax import lax
from jax.experimental import pallas as pl
from jax.experimental.pallas import tpu as pltpu
from jax.sharding import PartitionSpec as P

MESH = pl.DeviceIdType.MESH
TS = 32
ROWS = 128
CHUNK = 256
SINE = (3.1415820121765137, -5.167142868041992, 2.5418992042541504, -0.5546366572380066)
LEAD = SINE[-1]
MONIC = tuple(coef / LEAD for coef in SINE[:-1])
ATAN = (
    0.15915492177009583,
    -0.05305047705769539,
    0.031808558851480484,
    -0.022538291290402412,
    0.016709571704268456,
    -0.011514591053128242,
    0.006331328768283129,
    -0.0022920165210962296,
    0.00039099203422665596,
)
ONE = (1.0 + 6e-7) / (LEAD * LEAD)
HALF = 0.5 / (LEAD * LEAD)


def horner(coefs, y):
    total = jnp.float32(coefs[-1])
    for coef in coefs[-2::-1]:
        total = total * y + jnp.float32(coef)
    return total


def three_parts(value):
    first = value.astype(jnp.bfloat16).astype(jnp.float32)
    rest = value - first
    second = rest.astype(jnp.bfloat16).astype(jnp.float32)
    return first, second, rest - second


def polar(real, imag):
    wide, tall = jnp.abs(real), jnp.abs(imag)
    large, small = jnp.maximum(wide, tall), jnp.minimum(wide, tall)
    ratio = small / jnp.where(large > 0.0, large, 1.0)
    square = ratio * ratio
    size = large * jnp.sqrt(1.0 + square)
    angle = ratio * horner(ATAN, square)
    angle = jnp.where(tall > wide, 0.25 - angle, angle)
    angle = jnp.where(real < 0.0, 0.5 - angle, angle)
    return size, jnp.where(imag < 0.0, -angle, angle)


def nearest_first(own, step, count):
    spare = count - 1 - own
    reach = jnp.minimum(own, spare)
    half = (step + 1) // 2
    near = own + jnp.where(lax.rem(step, 2) == 1, -half, half)
    return jnp.where(step <= 2 * reach, near, jnp.where(own < spare, step, count - 1 - step))


def kernel(
    devices,
    chans,
    dirs,
    scale,
    tile_ref,
    channel_ref,
    position_ref,
    flux_ref,
    cluster_ref,
    jones_ref,
    uvw_ref,
    out_ref,
    st_send,
    st_recv,
    so_send,
    so_recv,
    table,
    feats,
    plain,
    weighted,
    rs_send,
    rs_recv,
    st_sent,
    st_came,
    so_sent,
    so_came,
    rs_sent,
    rs_came,
):
    me = lax.axis_index("src")
    rank = lax.rem(me, chans)
    planes = devices // chans
    plane = me // chans
    width = position_ref.shape[1]
    per_dev = uvw_ref.shape[1]
    parts = per_dev // 8
    per_group = ROWS // per_dev
    groups = devices // per_group
    group = me // per_group

    barrier = pltpu.get_barrier_semaphore()

    def greet(k, carry):
        there = lax.rem(me + k, devices)
        pl.semaphore_signal(barrier, inc=1, device_id={"src": there}, device_id_type=MESH)
        return carry

    lax.fori_loop(1, devices, greet, 0)

    lane = lax.broadcasted_iota(jnp.int32, (8, 128), 1)
    lane_group = lane // 32
    eight = lax.broadcasted_iota(jnp.int32, (8, per_dev), 0)
    coords = jnp.where(eight == 0, uvw_ref[0:1, :], 0.0)
    coords = jnp.where(eight == 1, uvw_ref[1:2, :], coords)
    coords = jnp.where(eight == 2, uvw_ref[2:3, :], coords)
    coords = jnp.concatenate([coords] * 16, 0).T
    features = []
    for c in range(chans):
        size, angle = polar(jones_ref[c, 0], jones_ref[c, 1])
        features += [-angle, (2.0 * LEAD * LEAD) * size]
    features = jnp.concatenate(features, 0).T

    def spread(pieces):
        total = pieces[0]
        for index, piece in enumerate(pieces[1:], 1):
            total = jnp.where(lane_group == index, piece, total)
        return total

    own_coords = spread([coords[8 * q : 8 * q + 8] for q in range(parts)])
    for c in range(chans):
        freq_ratio = 1.0 + 0.002 * channel_ref[c].astype(jnp.float32)
        pieces = [features[8 * q : 8 * q + 8] for q in range(parts)]
        pieces = [
            pltpu.roll(piece, (32 * (q - c)) % 128, 1) if q != c else piece
            for q, piece in enumerate(pieces)
        ]
        st_send[c, 0:8, :] = spread(pieces)
        st_send[c, 8:16, :] = own_coords * freq_ratio
    clusters = cluster_ref[...].astype(jnp.float32)
    for c in range(chans):
        so_send[c, 0:2, :] = position_ref[...]
        so_send[c, 2:3, :] = clusters
        so_send[c, 3:4, :] = flux_ref[c : c + 1, :]
    st_recv[me] = st_send[rank]
    so_recv[rank] = so_send[rank]

    pl.semaphore_wait(barrier, devices - 1)

    def source_copy(there_rank, slot):
        return pltpu.make_async_remote_copy(
            src_ref=so_send.at[there_rank],
            dst_ref=so_recv.at[slot],
            send_sem=so_sent.at[there_rank],
            recv_sem=so_came.at[slot],
            device_id={"src": plane * chans + there_rank},
            device_id_type=MESH,
        )

    def station_copy(there, slot):
        return pltpu.make_async_remote_copy(
            src_ref=st_send.at[lax.rem(there, chans)],
            dst_ref=st_recv.at[slot],
            send_sem=st_sent.at[there],
            recv_sem=st_came.at[slot],
            device_id={"src": there},
            device_id_type=MESH,
        )

    def result_copy(there, slot):
        return pltpu.make_async_remote_copy(
            src_ref=rs_send.at[there],
            dst_ref=rs_recv.at[slot],
            send_sem=rs_sent.at[there],
            recv_sem=rs_came.at[slot],
            device_id={"src": there},
            device_id_type=MESH,
        )

    for k in range(1, chans):
        there = lax.rem(rank + k, chans)
        source_copy(there, rank).start()
        station_copy(plane * chans + there, me).start()

    def send_stations(k, carry):
        there = nearest_first(plane, k // chans, planes) * chans + lax.rem(k, chans)
        station_copy(there, me).start()
        return carry

    lax.fori_loop(chans, devices, send_stations, 0)

    eight = lax.broadcasted_iota(jnp.int32, (8, width), 0)
    kinds = lax.broadcasted_iota(jnp.int32, (dirs, width), 0).astype(jnp.float32)

    def make_features(block, slot):
        cols = slice(block * width, block * width + width)
        l_row, m_row = so_recv[slot, 0:1, :], so_recv[slot, 1:2, :]
        n_row = jnp.sqrt(1.0 - l_row * l_row - m_row * m_row) - 1.0
        rows = jnp.where(eight == 0, l_row, jnp.where(eight == 1, m_row, 0.0))
        rows = jnp.where(eight == 2, n_row, rows)
        first, second, third = three_parts(rows)
        onehot = jnp.where(kinds == so_recv[slot, 2:3, :], 1.0, 0.0).astype(jnp.bfloat16)
        for index in range(4):
            feats[16 * index : 16 * index + 16, cols] = onehot
        pairs = ((first, second), (third, first), (second, first), (third, second))
        for index, pair in enumerate(pairs):
            at = 64 + 16 * index
            feats[at : at + 16, cols] = jnp.concatenate(pair, 0).astype(jnp.bfloat16)

    make_features(0, rank)
    for k in range(1, chans):
        slot = lax.rem(rank + k, chans)
        source_copy(rank, slot).wait_recv()
        make_features(k, slot)

    wide_lane = lax.broadcasted_iota(jnp.int32, (16, 128), 1)
    is_size = jnp.logical_and(wide_lane < 64, lax.rem(wide_lane, 32) >= 16)
    lane_slot = lax.rem(lane, 32) // 8

    def predict(step, carry):
        index = nearest_first(group, step, groups)
        blocks = []
        for j in range(per_group):
            there = index * per_group + j

            @pl.when(there != me)
            def _():
                station_copy(me, there).wait_recv()

            payload = st_recv[there]
            head, tail, _ = three_parts(payload[0:8])
            first, second, third = three_parts(payload[8:16])
            left = jnp.where(lane_slot == 3, second, first)
            right = jnp.where(lax.rem(lane_slot, 2) == 0, second, third)
            for q in range(parts):
                pieces = [
                    pltpu.roll(piece, (32 * (g - q)) % 128, 1) if g != q else piece
                    for g, piece in enumerate((head, tail, left, right))
                ]
                blocks.append(spread(pieces))
        for pair in range(ROWS // 16):
            value = jnp.concatenate(blocks[2 * pair : 2 * pair + 2], 0)
            at = 16 * pair
            table[at : at + 16, :] = jnp.where(is_size, 0.0, value).astype(jnp.bfloat16)
            below = ROWS + at
            table[below : below + 16, :] = jnp.where(is_size, value, 0.0).astype(jnp.bfloat16)

        for chunk in range(chans * width // CHUNK):
            begin = chunk * CHUNK
            cols = slice(begin, begin + CHUNK)
            slot = lax.rem(rank + begin // width, chans)
            inner = slice(begin % width, begin % width + CHUNK)
            weight = so_recv[slot, 3:4, inner] * scale
            found = jnp.dot(table[...], feats[:, cols], preferred_element_type=jnp.float32)
            for tile in range(ROWS // TS):
                turns = found[tile * TS : tile * TS + TS]
                double = found[ROWS + tile * TS : ROWS + tile * TS + TS]
                turns = turns - jnp.round(turns)
                square = turns * turns
                poly = square + jnp.float32(MONIC[2])
                poly = poly * square + jnp.float32(MONIC[1])
                poly = poly * square + jnp.float32(MONIC[0])
                sine = turns * poly
                square = sine * sine
                rest = ONE - square
                cosine = rest * lax.rsqrt(rest)
                real = double * (HALF - square)
                imag = (double * sine) * cosine
                at = index * (ROWS // TS) + tile
                plain[at, 0:TS, cols] = real.astype(jnp.bfloat16)
                plain[at, TS : 2 * TS, cols] = imag.astype(jnp.bfloat16)
                weighted[at, 0:TS, cols] = (real * weight).astype(jnp.bfloat16)
                weighted[at, TS : 2 * TS, cols] = (imag * weight).astype(jnp.bfloat16)
        return carry

    lax.fori_loop(0, groups, predict, 0)

    contract = (((1,), (1,)), ((), ()))

    def turned(value, shift):
        return pltpu.roll(value, (32 * shift) % 128, 1) if shift % 4 else value

    def owner_at(k):
        step = planes - 1 - k // chans
        return nearest_first(plane, step, planes) * chans + lax.rem(rank + 1 + k, chans)

    def send_result(there):
        @pl.when(there != me)
        def _():
            result_copy(there, me).start()

    def products(step, carry):
        for j in range(chans):
            k = step * chans + j
            owner = owner_at(k)
            left = weighted[tile_ref[0, owner]]
            right = plain[tile_ref[1, owner]]
            both = jnp.concatenate([right, right], 0)
            found = lax.dot_general(left, both, contract, preferred_element_type=jnp.float32)
            reals, imags = [], []
            for q in range(4):
                upper = found[8 * q : 8 * q + 8]
                lower = found[TS + 8 * q : TS + 8 * q + 8]
                reals.append(turned(upper, q) + turned(lower, q - 1))
                imags.append(turned(lower, q) - turned(upper, q - 1))
            rs_send[owner, 0:8, :] = spread(reals)
            rs_send[owner, 8:16, :] = spread(imags)
            if j:
                send_result(owner_at(k - 1))
            else:

                @pl.when(step > 0)
                def _():
                    send_result(owner_at(k - 1))

        return carry

    lax.fori_loop(0, planes, products, 0)

    def take(k, carry):
        there = lax.rem(me + k, devices)
        result_copy(me, there).wait_recv()
        return carry

    rs_recv[me] = rs_send[me]
    lax.fori_loop(1, devices, take, 0)

    same = tile_ref[0, me] == tile_ref[1, me]
    row = lax.broadcasted_iota(jnp.int32, (8, 128), 0)
    diagonal = row + 8 * lane_group == lax.rem(lane, 32)
    clear = jnp.logical_and(diagonal, same)
    for c in range(chans):
        total = rs_recv[c]
        for other in range(1, planes):
            total = total + rs_recv[other * chans + c]
        for part in range(2):
            value = jnp.where(clear, 0.0, total[8 * part : 8 * part + 8])
            for i in range(TS):
                out_ref[0, c, part : part + 1, i * TS : i * TS + TS] = value[
                    i % 8 : i % 8 + 1, i // 8 * TS : i // 8 * TS + TS
                ]

    def finish(k, carry):
        there = lax.rem(me + k, devices)
        station_copy(there, me).wait_send()
        result_copy(there, me).wait_send()
        return carry

    lax.fori_loop(1, devices, finish, 0)
    for k in range(1, chans):
        source_copy(lax.rem(rank + k, chans), rank).wait_send()


def on_device(positions, flux, cluster, jones, station_uvw, channels, tile_map):
    width = positions.shape[1]
    devices = lax.axis_size("src")
    scale = 1.0 / math.sqrt(width * devices)
    chans, _, dirs, per_dev = jones.shape
    tiles = devices * per_dev // TS

    vmem = pl.BlockSpec(memory_space=pltpu.VMEM)
    return pl.pallas_call(
        functools.partial(kernel, devices, chans, dirs, scale),
        out_shape=jax.ShapeDtypeStruct((1, chans, 2, TS * TS), jnp.float32),
        in_specs=[pl.BlockSpec(memory_space=pltpu.SMEM)] * 2 + [vmem] * 5,
        out_specs=vmem,
        scratch_shapes=[
            pltpu.VMEM((chans, 16, 128), jnp.float32),
            pltpu.VMEM((devices, 16, 128), jnp.float32),
            pltpu.VMEM((chans, 4, width), jnp.float32),
            pltpu.VMEM((chans, 4, width), jnp.float32),
            pltpu.VMEM((2 * ROWS, 128), jnp.bfloat16),
            pltpu.VMEM((128, chans * width), jnp.bfloat16),
            pltpu.VMEM((tiles, 2 * TS, chans * width), jnp.bfloat16),
            pltpu.VMEM((tiles, 2 * TS, chans * width), jnp.bfloat16),
            pltpu.VMEM((devices, 16, 128), jnp.float32),
            pltpu.VMEM((devices, 16, 128), jnp.float32),
            pltpu.SemaphoreType.DMA((devices,)),
            pltpu.SemaphoreType.DMA((devices,)),
            pltpu.SemaphoreType.DMA((chans,)),
            pltpu.SemaphoreType.DMA((chans,)),
            pltpu.SemaphoreType.DMA((devices,)),
            pltpu.SemaphoreType.DMA((devices,)),
        ],
        compiler_params=pltpu.CompilerParams(collective_id=0, has_side_effects=True),
    )(tile_map.T, channels, positions, flux, cluster[None], jones, station_uvw)


def solution(mesh):
    in_specs = (
        P(None, ("group", "src")),
        P(None, ("group", "src")),
        P(("group", "src")),
        P(None, None, None, ("group", "src")),
        P(None, ("group", "src")),
        P("group"),
        P("group", None),
    )
    out_specs = P(("group", "src"), None, None, None)
    return jax.shard_map(
        on_device, mesh=mesh, in_specs=in_specs, out_specs=out_specs, check_vma=False
    )
```

```python
import functools
import math

import jax
import jax.numpy as jnp
from jax import lax
from jax.experimental import pallas as pl
from jax.experimental.pallas import tpu as pltpu
from jax.sharding import PartitionSpec as P

MESH = pl.DeviceIdType.MESH
TS = 32
ROWS = 128
CHUNK = 256
SINE = (3.1415820121765137, -5.167142868041992, 2.5418992042541504, -0.5546366572380066)
LEAD = SINE[-1]
MONIC = tuple(coef / LEAD for coef in SINE[:-1])
ATAN = (
    0.15915492177009583,
    -0.05305047705769539,
    0.031808558851480484,
    -0.022538291290402412,
    0.016709571704268456,
    -0.011514591053128242,
    0.006331328768283129,
    -0.0022920165210962296,
    0.00039099203422665596,
)
ONE = (1.0 + 6e-7) / (LEAD * LEAD)
HALF = 0.5 / (LEAD * LEAD)


def horner(coefs, y):
    total = jnp.float32(coefs[-1])
    for coef in coefs[-2::-1]:
        total = total * y + jnp.float32(coef)
    return total


def three_parts(value):
    first = value.astype(jnp.bfloat16).astype(jnp.float32)
    rest = value - first
    second = rest.astype(jnp.bfloat16).astype(jnp.float32)
    return first, second, rest - second


def polar(real, imag):
    wide, tall = jnp.abs(real), jnp.abs(imag)
    large, small = jnp.maximum(wide, tall), jnp.minimum(wide, tall)
    ratio = small / jnp.where(large > 0.0, large, 1.0)
    square = ratio * ratio
    size = large * jnp.sqrt(1.0 + square)
    angle = ratio * horner(ATAN, square)
    angle = jnp.where(tall > wide, 0.25 - angle, angle)
    angle = jnp.where(real < 0.0, 0.5 - angle, angle)
    return size, jnp.where(imag < 0.0, -angle, angle)


def nearest_first(own, step, count):
    spare = count - 1 - own
    reach = jnp.minimum(own, spare)
    half = (step + 1) // 2
    near = own + jnp.where(lax.rem(step, 2) == 1, -half, half)
    return jnp.where(step <= 2 * reach, near, jnp.where(own < spare, step, count - 1 - step))


def kernel(
    devices,
    chans,
    dirs,
    scale,
    tile_in,
    channel_in,
    position_in,
    flux_in,
    cluster_in,
    jones_in,
    uvw_in,
    out_ref,
    tile_ref,
    channel_ref,
    position_ref,
    flux_ref,
    cluster_ref,
    jones_ref,
    uvw_ref,
    st_send,
    st_recv,
    so_send,
    so_recv,
    table,
    feats,
    plain,
    weighted,
    prods,
    rs_send,
    rs_recv,
    st_sent,
    st_came,
    so_sent,
    so_came,
    rs_sent,
    rs_came,
    loaded,
):
    me = lax.axis_index("src")
    rank = lax.rem(me, chans)
    planes = devices // chans
    plane = me // chans
    width = position_ref.shape[1]
    per_dev = uvw_ref.shape[1]
    parts = per_dev // 8
    per_group = ROWS // per_dev
    groups = devices // per_group
    group = me // per_group

    barrier = pltpu.get_barrier_semaphore()

    def greet(k, carry):
        there = lax.rem(me + k, devices)
        pl.semaphore_signal(barrier, inc=1, device_id={"src": there}, device_id_type=MESH)
        return carry

    lax.fori_loop(1, devices, greet, 0)

    loads = [
        pltpu.make_async_copy(source, target, loaded.at[index])
        for index, (source, target) in enumerate(
            (
                (jones_in, jones_ref),
                (uvw_in, uvw_ref),
                (channel_in, channel_ref),
                (position_in, position_ref),
                (flux_in, flux_ref),
                (cluster_in, cluster_ref),
                (tile_in, tile_ref),
            )
        )
    ]
    for load in loads:
        load.start()
    for load in loads:
        load.wait()

    lane = lax.broadcasted_iota(jnp.int32, (8, 128), 1)
    lane_group = lane // 32
    eight = lax.broadcasted_iota(jnp.int32, (8, per_dev), 0)
    coords = jnp.where(eight == 0, uvw_ref[0:1, :], 0.0)
    coords = jnp.where(eight == 1, uvw_ref[1:2, :], coords)
    coords = jnp.where(eight == 2, uvw_ref[2:3, :], coords)
    coords = jnp.concatenate([coords] * 16, 0).T
    features = []
    for c in range(chans):
        size, angle = polar(jones_ref[c, 0], jones_ref[c, 1])
        features += [-angle, (2.0 * LEAD * LEAD) * size]
    features = jnp.concatenate(features, 0).T

    def spread(pieces):
        total = pieces[0]
        for index, piece in enumerate(pieces[1:], 1):
            total = jnp.where(lane_group == index, piece, total)
        return total

    own_coords = spread([coords[8 * q : 8 * q + 8] for q in range(parts)])
    for c in range(chans):
        freq_ratio = 1.0 + 0.002 * channel_ref[c].astype(jnp.float32)
        pieces = [features[8 * q : 8 * q + 8] for q in range(parts)]
        pieces = [
            pltpu.roll(piece, (32 * (q - c)) % 128, 1) if q != c else piece
            for q, piece in enumerate(pieces)
        ]
        st_send[c, 0:8, :] = spread(pieces)
        st_send[c, 8:16, :] = own_coords * freq_ratio
    clusters = cluster_ref[...].astype(jnp.float32)
    for c in range(chans):
        so_send[c, 0:2, :] = position_ref[...]
        so_send[c, 2:3, :] = clusters
        so_send[c, 3:4, :] = flux_ref[c : c + 1, :]
    st_recv[me] = st_send[rank]
    so_recv[rank] = so_send[rank]

    pl.semaphore_wait(barrier, devices - 1)

    def source_copy(there_rank, slot):
        return pltpu.make_async_remote_copy(
            src_ref=so_send.at[there_rank],
            dst_ref=so_recv.at[slot],
            send_sem=so_sent.at[there_rank],
            recv_sem=so_came.at[slot],
            device_id={"src": plane * chans + there_rank},
            device_id_type=MESH,
        )

    def station_copy(there, slot):
        return pltpu.make_async_remote_copy(
            src_ref=st_send.at[lax.rem(there, chans)],
            dst_ref=st_recv.at[slot],
            send_sem=st_sent.at[there],
            recv_sem=st_came.at[slot],
            device_id={"src": there},
            device_id_type=MESH,
        )

    def result_copy(there, slot):
        return pltpu.make_async_remote_copy(
            src_ref=rs_send.at[there],
            dst_ref=rs_recv.at[slot],
            send_sem=rs_sent.at[there],
            recv_sem=rs_came.at[slot],
            device_id={"src": there},
            device_id_type=MESH,
        )

    for k in range(1, chans):
        there = lax.rem(rank + k, chans)
        source_copy(there, rank).start()
        station_copy(plane * chans + there, me).start()

    def send_stations(k, carry):
        there = nearest_first(plane, k // chans, planes) * chans + lax.rem(k, chans)
        station_copy(there, me).start()
        return carry

    lax.fori_loop(chans, devices, send_stations, 0)

    eight = lax.broadcasted_iota(jnp.int32, (8, width), 0)
    kinds = lax.broadcasted_iota(jnp.int32, (dirs, width), 0).astype(jnp.float32)

    def make_features(block, slot):
        l_row, m_row = so_recv[slot, 0:1, :], so_recv[slot, 1:2, :]
        n_row = jnp.sqrt(1.0 - l_row * l_row - m_row * m_row) - 1.0
        rows = jnp.where(eight == 0, l_row, jnp.where(eight == 1, m_row, 0.0))
        rows = jnp.where(eight == 2, n_row, rows)
        first, second, third = three_parts(rows)
        onehot = jnp.where(kinds == so_recv[slot, 2:3, :], 1.0, 0.0).astype(jnp.bfloat16)
        for index in range(4):
            feats[block, 16 * index : 16 * index + 16, :] = onehot
        pairs = ((first, second), (third, first), (second, first), (third, second))
        for index, pair in enumerate(pairs):
            at = 64 + 16 * index
            feats[block, at : at + 16, :] = jnp.concatenate(pair, 0).astype(jnp.bfloat16)

    make_features(0, rank)
    for k in range(1, chans):
        slot = lax.rem(rank + k, chans)
        source_copy(rank, slot).wait_recv()
        make_features(k, slot)

    wide_lane = lax.broadcasted_iota(jnp.int32, (16, 128), 1)
    is_size = jnp.logical_and(wide_lane < 64, lax.rem(wide_lane, 32) >= 16)
    lane_slot = lax.rem(lane, 32) // 8

    def make_table(step):
        index = nearest_first(group, step, groups)
        blocks = []
        for j in range(per_group):
            there = index * per_group + j

            @pl.when(there != me)
            def _():
                station_copy(me, there).wait_recv()

            payload = st_recv[there]
            head, tail, _ = three_parts(payload[0:8])
            first, second, third = three_parts(payload[8:16])
            left = jnp.where(lane_slot == 3, second, first)
            right = jnp.where(lax.rem(lane_slot, 2) == 0, second, third)
            for q in range(parts):
                pieces = [
                    pltpu.roll(piece, (32 * (g - q)) % 128, 1) if g != q else piece
                    for g, piece in enumerate((head, tail, left, right))
                ]
                blocks.append(spread(pieces))
        for pair in range(ROWS // 16):
            value = jnp.concatenate(blocks[2 * pair : 2 * pair + 2], 0)
            at = 16 * pair
            table[step, at : at + 16, :] = jnp.where(is_size, 0.0, value).astype(jnp.bfloat16)
            below = ROWS + at
            table[step, below : below + 16, :] = jnp.where(is_size, value, 0.0).astype(
                jnp.bfloat16
            )

    def predict(step, block, between=None):
        index = nearest_first(group, step, groups)
        slot = lax.rem(rank + block, chans)
        for chunk in range(width // CHUNK):
            cols = slice(chunk * CHUNK, chunk * CHUNK + CHUNK)
            weight = so_recv[slot, 3:4, cols] * scale
            found = jnp.dot(table[step], feats[block, :, cols], preferred_element_type=jnp.float32)
            for tile in range(ROWS // TS):
                turns = found[tile * TS : tile * TS + TS]
                double = found[ROWS + tile * TS : ROWS + tile * TS + TS]
                turns = turns - jnp.round(turns)
                square = turns * turns
                poly = square + jnp.float32(MONIC[2])
                poly = poly * square + jnp.float32(MONIC[1])
                poly = poly * square + jnp.float32(MONIC[0])
                sine = turns * poly
                square = sine * sine
                rest = ONE - square
                cosine = rest * lax.rsqrt(rest)
                real = double * (HALF - square)
                imag = (double * sine) * cosine
                at = index * (ROWS // TS) + tile
                plain[block][at, 0:TS, cols] = real.astype(jnp.bfloat16)
                plain[block][at, TS : 2 * TS, cols] = imag.astype(jnp.bfloat16)
                weighted[block][at, 0:TS, cols] = (real * weight).astype(jnp.bfloat16)
                weighted[block][at, TS : 2 * TS, cols] = (imag * weight).astype(jnp.bfloat16)
            if between is not None:
                between(chunk)

    contract = (((1,), (1,)), ((), ()))
    prods[...] = jnp.zeros_like(prods)

    def owner_at(k):
        step = planes - 1 - k // chans
        return nearest_first(plane, step, planes) * chans + lax.rem(rank + 1 + k, chans)

    def product(owner, block):
        left = weighted[block][tile_ref[0, owner]]
        right = plain[block][tile_ref[1, owner]]
        return lax.dot_general(left, right, contract, preferred_element_type=jnp.float32)

    make_table(0)
    for block in range(chans):
        predict(0, block)

    def first_step(step, carry):
        make_table(step)
        predict(step, 0)
        return carry

    lax.fori_loop(1, groups, first_step, 0)

    share = pl.cdiv(devices, groups - 1)

    def far_step(block, step, carry):
        def between(chunk):
            pieces = width // CHUNK
            for j in range(share * chunk // pieces, share * (chunk + 1) // pieces):
                k = step * share + j
                owner = owner_at(jnp.minimum(k, devices - 1))
                prods[k, :, 0 : 2 * TS] += product(owner, block)

        predict(step + 1, block + 1, between)
        return carry

    for block in range(chans - 1):
        lax.fori_loop(0, groups - 1, functools.partial(far_step, block), 0)

    def turned(value, shift):
        return pltpu.roll(value, (32 * shift) % 128, 1) if shift % 4 else value

    def finish_products(step):
        for j in range(chans):
            k = step * chans + j
            prods[k, :, 0 : 2 * TS] += product(owner_at(k), chans - 1)

    def pack(step):
        for j in range(chans):
            k = step * chans + j
            owner = owner_at(k)
            reals, imags = [], []
            for q in range(4):
                upper = prods[k, 8 * q : 8 * q + 8]
                lower = prods[k, TS + 8 * q : TS + 8 * q + 8]
                reals.append(turned(upper, q) + turned(lower, q - 1))
                imags.append(turned(lower, q) - turned(upper, q - 1))
            rs_send[owner, 0:8, :] = spread(reals)
            rs_send[owner, 8:16, :] = spread(imags)

    def last_step(step, carry):
        finish_products(step + 1)
        pack(step)
        for j in range(chans):
            result_copy(owner_at(step * chans + j), me).start()
        return carry

    finish_products(0)
    lax.fori_loop(0, planes - 1, last_step, 0)
    pack(planes - 1)
    for j in range(chans - 1):
        result_copy(owner_at(devices - chans + j), me).start()

    def take(k, carry):
        there = lax.rem(me + k, devices)
        result_copy(me, there).wait_recv()
        return carry

    rs_recv[me] = rs_send[me]
    lax.fori_loop(1, devices, take, 0)

    same = tile_ref[0, me] == tile_ref[1, me]
    row = lax.broadcasted_iota(jnp.int32, (8, 128), 0)
    diagonal = row + 8 * lane_group == lax.rem(lane, 32)
    clear = jnp.logical_and(diagonal, same)
    for c in range(chans):
        total = rs_recv[c]
        for other in range(1, planes):
            total = total + rs_recv[other * chans + c]
        for part in range(2):
            value = jnp.where(clear, 0.0, total[8 * part : 8 * part + 8])
            for i in range(TS):
                out_ref[0, c, part : part + 1, i * TS : i * TS + TS] = value[
                    i % 8 : i % 8 + 1, i // 8 * TS : i // 8 * TS + TS
                ]

    def finish(k, carry):
        there = lax.rem(me + k, devices)
        station_copy(there, me).wait_send()
        result_copy(there, me).wait_send()
        return carry

    lax.fori_loop(1, devices, finish, 0)
    for k in range(1, chans):
        source_copy(lax.rem(rank + k, chans), rank).wait_send()


def on_device(positions, flux, cluster, jones, station_uvw, channels, tile_map):
    width = positions.shape[1]
    devices = lax.axis_size("src")
    scale = 1.0 / math.sqrt(width * devices)
    chans, _, dirs, per_dev = jones.shape
    tiles = devices * per_dev // TS

    groups = devices * per_dev // ROWS
    share = pl.cdiv(devices, groups - 1)
    sides = [pltpu.VMEM((tiles, 2 * TS, width), jnp.bfloat16)] * chans
    cluster = cluster[None]
    tile_map = tile_map.T
    smem = [pltpu.SMEM(array.shape, array.dtype) for array in (tile_map, channels)]
    inputs = (positions, flux, cluster, jones, station_uvw)
    return pl.pallas_call(
        functools.partial(kernel, devices, chans, dirs, scale),
        out_shape=jax.ShapeDtypeStruct((1, chans, 2, TS * TS), jnp.float32),
        in_specs=[pl.BlockSpec(memory_space=pl.ANY)] * 7,
        out_specs=pl.BlockSpec(memory_space=pltpu.VMEM),
        scratch_shapes=smem
        + [pltpu.VMEM(array.shape, array.dtype) for array in inputs]
        + [
            pltpu.VMEM((chans, 16, 128), jnp.float32),
            pltpu.VMEM((devices, 16, 128), jnp.float32),
            pltpu.VMEM((chans, 4, width), jnp.float32),
            pltpu.VMEM((chans, 4, width), jnp.float32),
            pltpu.VMEM((groups, 2 * ROWS, 128), jnp.bfloat16),
            pltpu.VMEM((chans, 128, width), jnp.bfloat16),
            sides,
            sides,
            pltpu.VMEM((share * (groups - 1), 2 * TS, 128), jnp.float32),
            pltpu.VMEM((devices, 16, 128), jnp.float32),
            pltpu.VMEM((devices, 16, 128), jnp.float32),
            pltpu.SemaphoreType.DMA((devices,)),
            pltpu.SemaphoreType.DMA((devices,)),
            pltpu.SemaphoreType.DMA((chans,)),
            pltpu.SemaphoreType.DMA((chans,)),
            pltpu.SemaphoreType.DMA((devices,)),
            pltpu.SemaphoreType.DMA((devices,)),
            pltpu.SemaphoreType.DMA((7,)),
        ],
        compiler_params=pltpu.CompilerParams(collective_id=0, has_side_effects=True),
    )(tile_map, channels, *inputs)


def solution(mesh):
    in_specs = (
        P(None, ("group", "src")),
        P(None, ("group", "src")),
        P(("group", "src")),
        P(None, None, None, ("group", "src")),
        P(None, ("group", "src")),
        P("group"),
        P("group", None),
    )
    out_specs = P(("group", "src"), None, None, None)
    return jax.shard_map(
        on_device, mesh=mesh, in_specs=in_specs, out_specs=out_specs, check_vma=False
    )
```

```python
import functools
import math

import jax
import jax.numpy as jnp
from jax import lax
from jax.experimental import pallas as pl
from jax.experimental.pallas import tpu as pltpu
from jax.sharding import PartitionSpec as P

MESH = pl.DeviceIdType.MESH
TS = 32
ROWS = 128
CHUNK = 256
SINE = (3.1415820121765137, -5.167142868041992, 2.5418992042541504, -0.5546366572380066)
LEAD = SINE[-1]
MONIC = tuple(coef / LEAD for coef in SINE[:-1])
ATAN = (
    0.15915492177009583,
    -0.05305047705769539,
    0.031808558851480484,
    -0.022538291290402412,
    0.016709571704268456,
    -0.011514591053128242,
    0.006331328768283129,
    -0.0022920165210962296,
    0.00039099203422665596,
)
ONE = (1.0 + 6e-7) / (LEAD * LEAD)
HALF = 0.5 / (LEAD * LEAD)


def horner(coefs, y):
    total = jnp.float32(coefs[-1])
    for coef in coefs[-2::-1]:
        total = total * y + jnp.float32(coef)
    return total


def three_parts(value):
    first = value.astype(jnp.bfloat16).astype(jnp.float32)
    rest = value - first
    second = rest.astype(jnp.bfloat16).astype(jnp.float32)
    return first, second, rest - second


def polar(real, imag):
    wide, tall = jnp.abs(real), jnp.abs(imag)
    large, small = jnp.maximum(wide, tall), jnp.minimum(wide, tall)
    ratio = small / jnp.where(large > 0.0, large, 1.0)
    square = ratio * ratio
    size = large * jnp.sqrt(1.0 + square)
    angle = ratio * horner(ATAN, square)
    angle = jnp.where(tall > wide, 0.25 - angle, angle)
    angle = jnp.where(real < 0.0, 0.5 - angle, angle)
    return size, jnp.where(imag < 0.0, -angle, angle)


def nearest_first(own, step, count):
    spare = count - 1 - own
    reach = jnp.minimum(own, spare)
    half = (step + 1) // 2
    near = own + jnp.where(lax.rem(step, 2) == 1, -half, half)
    return jnp.where(step <= 2 * reach, near, jnp.where(own < spare, step, count - 1 - step))


def kernel(
    devices,
    chans,
    dirs,
    scale,
    tile_in,
    channel_in,
    position_in,
    flux_in,
    cluster_in,
    jones_in,
    uvw_in,
    out_ref,
    tile_ref,
    channel_ref,
    position_ref,
    flux_ref,
    cluster_ref,
    jones_ref,
    uvw_ref,
    st_send,
    st_recv,
    so_send,
    so_recv,
    table,
    feats,
    plain,
    weighted,
    prods,
    rs_send,
    rs_recv,
    st_sent,
    st_came,
    so_sent,
    so_came,
    rs_sent,
    rs_came,
    loaded,
):
    me = lax.axis_index("src")
    rank = lax.rem(me, chans)
    planes = devices // chans
    plane = me // chans
    width = position_ref.shape[1]
    per_dev = uvw_ref.shape[1]
    parts = per_dev // 8
    per_group = ROWS // per_dev
    groups = devices // per_group
    group = me // per_group

    barrier = pltpu.get_barrier_semaphore()

    loads = [
        pltpu.make_async_copy(source, target, loaded.at[index])
        for index, (source, target) in enumerate(
            (
                (jones_in, jones_ref),
                (uvw_in, uvw_ref),
                (channel_in, channel_ref),
                (position_in, position_ref),
                (flux_in, flux_ref),
                (cluster_in, cluster_ref),
                (tile_in, tile_ref),
            )
        )
    ]
    for load in loads:
        load.start()

    def greet(k, carry):
        there = lax.rem(me + k, devices)
        pl.semaphore_signal(barrier, inc=1, device_id={"src": there}, device_id_type=MESH)
        return carry

    lax.fori_loop(1, devices, greet, 0)

    for load in loads:
        load.wait()

    lane = lax.broadcasted_iota(jnp.int32, (8, 128), 1)
    lane_group = lane // 32
    eight = lax.broadcasted_iota(jnp.int32, (8, per_dev), 0)
    coords = jnp.where(eight == 0, uvw_ref[0:1, :], 0.0)
    coords = jnp.where(eight == 1, uvw_ref[1:2, :], coords)
    coords = jnp.where(eight == 2, uvw_ref[2:3, :], coords)
    coords = jnp.concatenate([coords] * 16, 0).T
    features = []
    for c in range(chans):
        size, angle = polar(jones_ref[c, 0], jones_ref[c, 1])
        features += [-angle, (2.0 * LEAD * LEAD) * size]
    features = jnp.concatenate(features, 0).T

    def spread(pieces):
        total = pieces[0]
        for index, piece in enumerate(pieces[1:], 1):
            total = jnp.where(lane_group == index, piece, total)
        return total

    own_coords = spread([coords[8 * q : 8 * q + 8] for q in range(parts)])
    for c in range(chans):
        freq_ratio = 1.0 + 0.002 * channel_ref[c].astype(jnp.float32)
        pieces = [features[8 * q : 8 * q + 8] for q in range(parts)]
        pieces = [
            pltpu.roll(piece, (32 * (q - c)) % 128, 1) if q != c else piece
            for q, piece in enumerate(pieces)
        ]
        st_send[c, 0:8, :] = spread(pieces)
        st_send[c, 8:16, :] = own_coords * freq_ratio
    clusters = cluster_ref[...].astype(jnp.float32)
    for c in range(chans):
        so_send[c, 0:2, :] = position_ref[...]
        so_send[c, 2:3, :] = clusters
        so_send[c, 3:4, :] = flux_ref[c : c + 1, :]
    st_recv[me] = st_send[rank]
    so_recv[rank] = so_send[rank]

    pl.semaphore_wait(barrier, devices - 1)

    def source_copy(there_rank, slot):
        return pltpu.make_async_remote_copy(
            src_ref=so_send.at[there_rank],
            dst_ref=so_recv.at[slot],
            send_sem=so_sent.at[there_rank],
            recv_sem=so_came.at[slot],
            device_id={"src": plane * chans + there_rank},
            device_id_type=MESH,
        )

    def station_copy(there, slot):
        return pltpu.make_async_remote_copy(
            src_ref=st_send.at[lax.rem(there, chans)],
            dst_ref=st_recv.at[slot],
            send_sem=st_sent.at[there],
            recv_sem=st_came.at[slot],
            device_id={"src": there},
            device_id_type=MESH,
        )

    def result_copy(there, slot):
        return pltpu.make_async_remote_copy(
            src_ref=rs_send.at[there],
            dst_ref=rs_recv.at[slot],
            send_sem=rs_sent.at[there],
            recv_sem=rs_came.at[slot],
            device_id={"src": there},
            device_id_type=MESH,
        )

    for k in range(1, chans):
        there = lax.rem(rank + k, chans)
        source_copy(there, rank).start()
        station_copy(plane * chans + there, me).start()

    def send_stations(k, carry):
        there = nearest_first(plane, k // chans, planes) * chans + lax.rem(k, chans)
        station_copy(there, me).start()
        return carry

    lax.fori_loop(chans, devices, send_stations, 0)

    eight = lax.broadcasted_iota(jnp.int32, (8, width), 0)
    kinds = lax.broadcasted_iota(jnp.int32, (dirs, width), 0).astype(jnp.float32)

    def make_features(block, slot):
        l_row, m_row = so_recv[slot, 0:1, :], so_recv[slot, 1:2, :]
        n_row = jnp.sqrt(1.0 - l_row * l_row - m_row * m_row) - 1.0
        rows = jnp.where(eight == 0, l_row, jnp.where(eight == 1, m_row, 0.0))
        rows = jnp.where(eight == 2, n_row, rows)
        first, second, third = three_parts(rows)
        onehot = jnp.where(kinds == so_recv[slot, 2:3, :], 1.0, 0.0).astype(jnp.bfloat16)
        pieces = [(16 * index, onehot) for index in range(4)]
        pairs = ((first, second), (third, first), (second, first), (third, second))
        for index, pair in enumerate(pairs):
            pieces.append((64 + 16 * index, jnp.concatenate(pair, 0).astype(jnp.bfloat16)))
        for at, piece in pieces:
            for lanes in range(width // 128):
                feats[block, lanes, at : at + 16, :] = piece[:, 128 * lanes : 128 * lanes + 128]

    make_features(0, rank)
    for k in range(1, chans):
        slot = lax.rem(rank + k, chans)
        source_copy(rank, slot).wait_recv()
        make_features(k, slot)

    wide_lane = lax.broadcasted_iota(jnp.int32, (16, 128), 1)
    is_size = jnp.logical_and(wide_lane < 64, lax.rem(wide_lane, 32) >= 16)
    lane_slot = lax.rem(lane, 32) // 8

    def await_group(step):
        index = nearest_first(group, step, groups)
        for j in range(per_group):
            there = index * per_group + j
            if step:
                station_copy(me, there).wait_recv()
            else:

                @pl.when(there != me)
                def _():
                    station_copy(me, there).wait_recv()

    def make_table(step):
        index = nearest_first(group, step, groups)
        blocks = []
        for j in range(per_group):
            there = index * per_group + j
            payload = st_recv[there]
            head, tail, _ = three_parts(payload[0:8])
            first, second, third = three_parts(payload[8:16])
            left = jnp.where(lane_slot == 3, second, first)
            right = jnp.where(lax.rem(lane_slot, 2) == 0, second, third)
            for q in range(parts):
                pieces = [
                    pltpu.roll(piece, (32 * (g - q)) % 128, 1) if g != q else piece
                    for g, piece in enumerate((head, tail, left, right))
                ]
                blocks.append(spread(pieces))
        for pair in range(ROWS // 16):
            value = jnp.concatenate(blocks[2 * pair : 2 * pair + 2], 0)
            at = 16 * pair
            table[step, at : at + 16, :] = jnp.where(is_size, 0.0, value).astype(jnp.bfloat16)
            below = ROWS + at
            table[step, below : below + 16, :] = jnp.where(is_size, value, 0.0).astype(
                jnp.bfloat16
            )

    def predict(step, block, between=None):
        index = nearest_first(group, step, groups)
        slot = lax.rem(rank + block, chans)
        for chunk in range(width // CHUNK):
            cols = slice(chunk * CHUNK, chunk * CHUNK + CHUNK)
            weight = so_recv[slot, 3:4, cols] * scale
            begin = chunk * (CHUNK // 128)
            wide = [feats[block, begin + index] for index in range(CHUNK // 128)]
            found = jnp.dot(
                table[step], jnp.concatenate(wide, 1), preferred_element_type=jnp.float32
            )
            for tile in range(ROWS // TS):
                turns = found[tile * TS : tile * TS + TS]
                double = found[ROWS + tile * TS : ROWS + tile * TS + TS]
                turns = turns - jnp.round(turns)
                square = turns * turns
                poly = square + jnp.float32(MONIC[2])
                poly = poly * square + jnp.float32(MONIC[1])
                poly = poly * square + jnp.float32(MONIC[0])
                sine = turns * poly
                square = sine * sine
                rest = ONE - square
                cosine = rest * lax.rsqrt(rest)
                real = double * (HALF - square)
                imag = (double * sine) * cosine
                at = index * (ROWS // TS) + tile
                results = (
                    (plain[block], 0, real),
                    (plain[block], TS, imag),
                    (weighted[block], 0, real * weight),
                    (weighted[block], TS, imag * weight),
                )
                for side, top, value in results:
                    value = value.astype(jnp.bfloat16)
                    for index_in in range(CHUNK // 128):
                        side[at, begin + index_in, top : top + TS, :] = value[
                            :, 128 * index_in : 128 * index_in + 128
                        ]
            if between is not None:
                between(chunk)

    contract = (((1,), (1,)), ((), ()))
    prods[...] = jnp.zeros_like(prods)

    def owner_at(k):
        step = planes - 1 - k // chans
        return nearest_first(plane, step, planes) * chans + lax.rem(rank + 1 + k, chans)

    def product(owner, block):
        first, second = tile_ref[0, owner], tile_ref[1, owner]
        lanes = range(width // 128)
        left = jnp.concatenate([weighted[block][first, index] for index in lanes], 1)
        right = jnp.concatenate([plain[block][second, index] for index in lanes], 1)
        return lax.dot_general(left, right, contract, preferred_element_type=jnp.float32)

    await_group(0)
    make_table(0)
    for block in range(chans - 1):
        predict(0, block)
    for step in range(groups):
        if step + 1 < groups:
            await_group(step + 1)
            make_table(step + 1)
        predict(step, 0 if step else chans - 1)

    slots = (groups - 1) * (width // CHUNK)

    def between(block, turn):
        for k in range(devices * turn // slots, devices * (turn + 1) // slots):
            prods[k, :, 0 : 2 * TS] += product(owner_at(k), block)

    for block in range(chans - 1):
        for step in range(1, groups):
            base = (step - 1) * (width // CHUNK)
            predict(step, block + 1, lambda chunk: between(block, base + chunk))

    def turned(value, shift):
        return pltpu.roll(value, (32 * shift) % 128, 1) if shift % 4 else value

    def finish_products(step):
        for j in range(chans):
            k = step * chans + j
            prods[k, :, 0 : 2 * TS] += product(owner_at(k), chans - 1)

    def pack(step):
        for j in range(chans):
            k = step * chans + j
            owner = owner_at(k)
            reals, imags = [], []
            for q in range(4):
                upper = prods[k, 8 * q : 8 * q + 8]
                lower = prods[k, TS + 8 * q : TS + 8 * q + 8]
                reals.append(turned(upper, q) + turned(lower, q - 1))
                imags.append(turned(lower, q) - turned(upper, q - 1))
            rs_send[owner, 0:8, :] = spread(reals)
            rs_send[owner, 8:16, :] = spread(imags)

    def last_step(step, carry):
        finish_products(step + 1)
        pack(step)
        for j in range(chans):
            result_copy(owner_at(step * chans + j), me).start()
        return carry

    finish_products(0)
    lax.fori_loop(0, planes - 1, last_step, 0)
    pack(planes - 1)
    for j in range(chans - 1):
        result_copy(owner_at(devices - chans + j), me).start()

    def finish(k, carry):
        there = lax.rem(me + k, devices)
        station_copy(there, me).wait_send()
        result_copy(there, me).wait_send()
        return carry

    lax.fori_loop(1, devices, finish, 0)
    for k in range(1, chans):
        source_copy(lax.rem(rank + k, chans), rank).wait_send()

    def take(k, carry):
        there = lax.rem(me + k, devices)
        result_copy(me, there).wait_recv()
        return carry

    rs_recv[me] = rs_send[me]
    lax.fori_loop(1, devices, take, 0)

    same = tile_ref[0, me] == tile_ref[1, me]
    row = lax.broadcasted_iota(jnp.int32, (8, 128), 0)
    diagonal = row + 8 * lane_group == lax.rem(lane, 32)
    clear = jnp.logical_and(diagonal, same)
    lines = lax.rem(row, 4) == lane_group
    for c in range(chans):
        total = rs_recv[c]
        for other in range(1, planes):
            total = total + rs_recv[other * chans + c]
        for part in range(2):
            value = jnp.where(clear, 0.0, total[8 * part : 8 * part + 8])
            shifted = [turned(value, shift) for shift in range(4)]
            for q in range(4):
                piece = shifted[(4 - q) % 4]
                for other in range(1, 4):
                    piece = jnp.where(lane_group == other, shifted[(other - q) % 4], piece)
                piece = jnp.where(lines, piece, 0.0)
                for half in range(2):
                    line = jnp.sum(piece[4 * half : 4 * half + 4], 0, keepdims=True)
                    at = 128 * (2 * q + half)
                    out_ref[0, c, part : part + 1, at : at + 128] = line


def on_device(positions, flux, cluster, jones, station_uvw, channels, tile_map):
    width = positions.shape[1]
    devices = lax.axis_size("src")
    scale = 1.0 / math.sqrt(width * devices)
    chans, _, dirs, per_dev = jones.shape
    tiles = devices * per_dev // TS

    groups = devices * per_dev // ROWS
    sides = [pltpu.VMEM((tiles, width // 128, 2 * TS, 128), jnp.bfloat16)] * chans
    cluster = cluster[None]
    tile_map = tile_map.T
    smem = [pltpu.SMEM(array.shape, array.dtype) for array in (tile_map, channels)]
    inputs = (positions, flux, cluster, jones, station_uvw)
    return pl.pallas_call(
        functools.partial(kernel, devices, chans, dirs, scale),
        out_shape=pltpu.VMEM((1, chans, 2, TS * TS), jnp.float32),
        in_specs=[pl.BlockSpec(memory_space=pl.ANY)] * 7,
        out_specs=pl.BlockSpec(memory_space=pltpu.VMEM),
        scratch_shapes=smem
        + [pltpu.VMEM(array.shape, array.dtype) for array in inputs]
        + [
            pltpu.VMEM((chans, 16, 128), jnp.float32),
            pltpu.VMEM((devices, 16, 128), jnp.float32),
            pltpu.VMEM((chans, 4, width), jnp.float32),
            pltpu.VMEM((chans, 4, width), jnp.float32),
            pltpu.VMEM((groups, 2 * ROWS, 128), jnp.bfloat16),
            pltpu.VMEM((chans, width // 128, 128, 128), jnp.bfloat16),
            sides,
            sides,
            pltpu.VMEM((devices, 2 * TS, 128), jnp.float32),
            pltpu.VMEM((devices, 16, 128), jnp.float32),
            pltpu.VMEM((devices, 16, 128), jnp.float32),
            pltpu.SemaphoreType.DMA((devices,)),
            pltpu.SemaphoreType.DMA((devices,)),
            pltpu.SemaphoreType.DMA((chans,)),
            pltpu.SemaphoreType.DMA((chans,)),
            pltpu.SemaphoreType.DMA((devices,)),
            pltpu.SemaphoreType.DMA((devices,)),
            pltpu.SemaphoreType.DMA((7,)),
        ],
        compiler_params=pltpu.CompilerParams(collective_id=0, has_side_effects=True),
    )(tile_map, channels, *inputs)


def solution(mesh):
    in_specs = (
        P(None, ("group", "src")),
        P(None, ("group", "src")),
        P(("group", "src")),
        P(None, None, None, ("group", "src")),
        P(None, ("group", "src")),
        P("group"),
        P("group", None),
    )
    out_specs = P(("group", "src"), None, None, None)
    return jax.shard_map(
        on_device, mesh=mesh, in_specs=in_specs, out_specs=out_specs, check_vma=False
    )
```

```python
import functools
import math

import jax
import jax.numpy as jnp
from jax import lax
from jax.experimental import pallas as pl
from jax.experimental.pallas import tpu as pltpu
from jax.sharding import PartitionSpec as P

MESH = pl.DeviceIdType.MESH
TS = 32
ROWS = 128
CHUNK = 256
SINE = (3.1415820121765137, -5.167142868041992, 2.5418992042541504, -0.5546366572380066)
LEAD = SINE[-1]
MONIC = tuple(coef / LEAD for coef in SINE[:-1])
ATAN = (
    0.15915492177009583,
    -0.05305047705769539,
    0.031808558851480484,
    -0.022538291290402412,
    0.016709571704268456,
    -0.011514591053128242,
    0.006331328768283129,
    -0.0022920165210962296,
    0.00039099203422665596,
)
ONE = (1.0 + 6e-7) / (LEAD * LEAD)
HALF = 0.5 / (LEAD * LEAD)


def horner(coefs, y):
    total = jnp.float32(coefs[-1])
    for coef in coefs[-2::-1]:
        total = total * y + jnp.float32(coef)
    return total


def three_parts(value):
    first = value.astype(jnp.bfloat16).astype(jnp.float32)
    rest = value - first
    second = rest.astype(jnp.bfloat16).astype(jnp.float32)
    return first, second, rest - second


def polar(real, imag):
    wide, tall = jnp.abs(real), jnp.abs(imag)
    large, small = jnp.maximum(wide, tall), jnp.minimum(wide, tall)
    ratio = small / jnp.where(large > 0.0, large, 1.0)
    square = ratio * ratio
    size = large * jnp.sqrt(1.0 + square)
    angle = ratio * horner(ATAN, square)
    angle = jnp.where(tall > wide, 0.25 - angle, angle)
    angle = jnp.where(real < 0.0, 0.5 - angle, angle)
    return size, jnp.where(imag < 0.0, -angle, angle)


def nearest_first(own, step, count):
    spare = count - 1 - own
    reach = jnp.minimum(own, spare)
    half = (step + 1) // 2
    near = own + jnp.where(lax.rem(step, 2) == 1, -half, half)
    return jnp.where(step <= 2 * reach, near, jnp.where(own < spare, step, count - 1 - step))


def kernel(
    devices,
    chans,
    dirs,
    scale,
    tile_in,
    channel_in,
    position_in,
    flux_in,
    cluster_in,
    jones_in,
    uvw_in,
    out_ref,
    tile_ref,
    channel_ref,
    position_ref,
    flux_ref,
    cluster_ref,
    jones_ref,
    uvw_ref,
    st_send,
    st_recv,
    so_send,
    so_recv,
    table,
    feats,
    plain,
    weighted,
    prods,
    rs_send,
    rs_recv,
    st_sent,
    st_came,
    so_sent,
    so_came,
    rs_sent,
    rs_came,
    loaded,
    ready,
):
    me = lax.axis_index("src")
    rank = lax.rem(me, chans)
    planes = devices // chans
    plane = me // chans
    width = position_ref.shape[1]
    per_dev = uvw_ref.shape[1]
    parts = per_dev // 8
    per_group = ROWS // per_dev
    groups = devices // per_group
    group = me // per_group

    def slot_of(block):
        outer = lax.rem(rank // 2 + block // 2, chans // 2)
        return 2 * outer + lax.rem(rank + block, 2)

    barrier = pltpu.get_barrier_semaphore()

    loads = [
        pltpu.make_async_copy(source, target, loaded.at[index])
        for index, (source, target) in enumerate(
            (
                (jones_in, jones_ref),
                (uvw_in, uvw_ref),
                (channel_in, channel_ref),
                (position_in, position_ref),
                (flux_in, flux_ref),
                (cluster_in, cluster_ref),
                (tile_in, tile_ref),
            )
        )
    ]
    for load in loads:
        load.start()

    def greet(there, carry):
        @pl.when(there != me)
        def _():
            pl.semaphore_signal(barrier, inc=1, device_id={"src": there}, device_id_type=MESH)

        return carry

    lax.fori_loop(plane * chans, devices, greet, 0)
    pl.semaphore_wait(barrier, plane * chans + chans - 1)

    def answer(there, carry):
        pl.semaphore_signal(
            ready.at[plane], inc=1, device_id={"src": there}, device_id_type=MESH
        )
        return carry

    lax.fori_loop(0, plane * chans, answer, 0)

    for load in loads:
        load.wait()

    lane = lax.broadcasted_iota(jnp.int32, (8, 128), 1)
    lane_group = lane // 32
    eight = lax.broadcasted_iota(jnp.int32, (8, per_dev), 0)
    coords = jnp.where(eight == 0, uvw_ref[0:1, :], 0.0)
    coords = jnp.where(eight == 1, uvw_ref[1:2, :], coords)
    coords = jnp.where(eight == 2, uvw_ref[2:3, :], coords)
    coords = jnp.concatenate([coords] * 16, 0).T
    features = []
    for c in range(chans):
        size, angle = polar(jones_ref[c, 0], jones_ref[c, 1])
        features += [-angle, (2.0 * LEAD * LEAD) * size]
    features = jnp.concatenate(features, 0).T

    def spread(pieces):
        total = pieces[0]
        for index, piece in enumerate(pieces[1:], 1):
            total = jnp.where(lane_group == index, piece, total)
        return total

    own_coords = spread([coords[8 * q : 8 * q + 8] for q in range(parts)])
    for c in range(chans):
        freq_ratio = 1.0 + 0.002 * channel_ref[c].astype(jnp.float32)
        pieces = [features[8 * q : 8 * q + 8] for q in range(parts)]
        pieces = [
            pltpu.roll(piece, (32 * (q - c)) % 128, 1) if q != c else piece
            for q, piece in enumerate(pieces)
        ]
        st_send[c, 0:8, :] = spread(pieces)
        st_send[c, 8:16, :] = own_coords * freq_ratio
    clusters = cluster_ref[...].astype(jnp.float32)
    for c in range(chans):
        so_send[c, 0:2, :] = position_ref[...]
        so_send[c, 2:3, :] = clusters
        so_send[c, 3:4, :] = flux_ref[c : c + 1, :]
    st_recv[me] = st_send[rank]
    so_recv[rank] = so_send[rank]

    def source_copy(there_rank, slot):
        return pltpu.make_async_remote_copy(
            src_ref=so_send.at[there_rank],
            dst_ref=so_recv.at[slot],
            send_sem=so_sent.at[there_rank],
            recv_sem=so_came.at[slot],
            device_id={"src": plane * chans + there_rank},
            device_id_type=MESH,
        )

    def station_copy(there, slot):
        return pltpu.make_async_remote_copy(
            src_ref=st_send.at[lax.rem(there, chans)],
            dst_ref=st_recv.at[slot],
            send_sem=st_sent.at[there],
            recv_sem=st_came.at[slot],
            device_id={"src": there},
            device_id_type=MESH,
        )

    def result_copy(there, slot):
        return pltpu.make_async_remote_copy(
            src_ref=rs_send.at[there],
            dst_ref=rs_recv.at[slot],
            send_sem=rs_sent.at[there],
            recv_sem=rs_came.at[slot],
            device_id={"src": there},
            device_id_type=MESH,
        )

    for k in range(1, chans):
        there = slot_of(k)
        source_copy(there, rank).start()
        station_copy(plane * chans + there, me).start()

    def send_stations(there, carry):
        station_copy(there, me).start()
        return carry

    def send_above(above, carry):
        pl.semaphore_wait(ready.at[above], chans)
        return lax.fori_loop(above * chans, above * chans + chans, send_stations, carry)

    lax.fori_loop(0, plane * chans, send_stations, 0)

    eight = lax.broadcasted_iota(jnp.int32, (8, width), 0)
    kinds = lax.broadcasted_iota(jnp.int32, (dirs, width), 0).astype(jnp.float32)

    def make_features(block, slot):
        l_row, m_row = so_recv[slot, 0:1, :], so_recv[slot, 1:2, :]
        n_row = jnp.sqrt(1.0 - l_row * l_row - m_row * m_row) - 1.0
        rows = jnp.where(eight == 0, l_row, jnp.where(eight == 1, m_row, 0.0))
        rows = jnp.where(eight == 2, n_row, rows)
        first, second, third = three_parts(rows)
        onehot = jnp.where(kinds == so_recv[slot, 2:3, :], 1.0, 0.0).astype(jnp.bfloat16)
        pieces = [(16 * index, onehot) for index in range(4)]
        pairs = ((first, second), (third, first), (second, first), (third, second))
        for index, pair in enumerate(pairs):
            pieces.append((64 + 16 * index, jnp.concatenate(pair, 0).astype(jnp.bfloat16)))
        for at, piece in pieces:
            for lanes in range(width // 128):
                feats[block, lanes, at : at + 16, :] = piece[:, 128 * lanes : 128 * lanes + 128]

    def take_source(block):
        slot = slot_of(block)
        if block:
            source_copy(rank, slot).wait_recv()
        make_features(block, slot)

    take_source(0)
    take_source(1)

    wide_lane = lax.broadcasted_iota(jnp.int32, (16, 128), 1)
    is_size = jnp.logical_and(wide_lane < 64, lax.rem(wide_lane, 32) >= 16)
    lane_slot = lax.rem(lane, 32) // 8

    part_devices = per_group // 2
    own_part = lax.rem(me, per_group) // part_devices

    def await_part(step, part):
        first_device = nearest_first(group, step, groups) * per_group + part * part_devices
        for j in range(part_devices):
            there = first_device + j
            if step:
                station_copy(me, there).wait_recv()
            else:

                @pl.when(there != me)
                def _():
                    station_copy(me, there).wait_recv()

    def make_table(step, part):
        first_device = nearest_first(group, step, groups) * per_group + part * part_devices
        blocks = []
        for j in range(part_devices):
            payload = st_recv[first_device + j]
            head, tail, _ = three_parts(payload[0:8])
            first, second, third = three_parts(payload[8:16])
            left = jnp.where(lane_slot == 3, second, first)
            right = jnp.where(lax.rem(lane_slot, 2) == 0, second, third)
            for q in range(parts):
                pieces = [
                    pltpu.roll(piece, (32 * (g - q)) % 128, 1) if g != q else piece
                    for g, piece in enumerate((head, tail, left, right))
                ]
                blocks.append(spread(pieces))
        for pair in range(ROWS // 32):
            value = jnp.concatenate(blocks[2 * pair : 2 * pair + 2], 0)
            at = 16 * pair
            table[step, part, at : at + 16, :] = jnp.where(is_size, 0.0, value).astype(
                jnp.bfloat16
            )
            below = ROWS // 2 + at
            table[step, part, below : below + 16, :] = jnp.where(is_size, value, 0.0).astype(
                jnp.bfloat16
            )

    def predict(step, block, part=None, between=None):
        base = nearest_first(group, step, groups) * (ROWS // TS)
        slot = slot_of(block)
        if part is None:
            rows = jnp.concatenate([table[step, 0], table[step, 1]], 0)
        else:
            rows = table[step, part]
            base = base + part * (ROWS // TS // 2)
        for chunk in range(width // CHUNK):
            cols = slice(chunk * CHUNK, chunk * CHUNK + CHUNK)
            weight = so_recv[slot, 3:4, cols] * scale
            begin = chunk * (CHUNK // 128)
            wide = [feats[block, begin + index] for index in range(CHUNK // 128)]
            found = jnp.dot(rows, jnp.concatenate(wide, 1), preferred_element_type=jnp.float32)
            for tile in range(rows.shape[0] // (2 * TS)):
                top = tile // 2 * ROWS + tile % 2 * TS
                turns = found[top : top + TS]
                double = found[top + ROWS // 2 : top + ROWS // 2 + TS]
                turns = turns - jnp.round(turns)
                square = turns * turns
                poly = square + jnp.float32(MONIC[2])
                poly = poly * square + jnp.float32(MONIC[1])
                poly = poly * square + jnp.float32(MONIC[0])
                sine = turns * poly
                square = sine * sine
                rest = ONE - square
                cosine = rest * lax.rsqrt(rest)
                real = double * (HALF - square)
                imag = (double * sine) * cosine
                at = base + tile
                results = (
                    (plain[block], 0, real),
                    (plain[block], TS, imag),
                    (weighted[block], 0, real * weight),
                    (weighted[block], TS, imag * weight),
                )
                for side, top, value in results:
                    value = value.astype(jnp.bfloat16)
                    for index_in in range(CHUNK // 128):
                        side[at, begin + index_in, top : top + TS, :] = value[
                            :, 128 * index_in : 128 * index_in + 128
                        ]
            if between is not None:
                between(chunk)

    contract = (((1,), (1,)), ((), ()))
    prods[...] = jnp.zeros_like(prods)

    def product(owner, block):
        first, second = tile_ref[0, owner], tile_ref[1, owner]
        lanes = range(width // 128)
        left = jnp.concatenate([weighted[block][first, index] for index in lanes], 1)
        right = jnp.concatenate([plain[block][second, index] for index in lanes], 1)
        return lax.dot_general(left, right, contract, preferred_element_type=jnp.float32)

    await_part(0, own_part)
    make_table(0, own_part)
    predict(0, 0, own_part)
    predict(0, 1, own_part)
    lax.fori_loop(plane + 1, planes, send_above, 0)
    await_part(0, 1 - own_part)
    make_table(0, 1 - own_part)
    for block in range(2, chans):
        take_source(block)
    predict(0, 0, 1 - own_part)
    predict(0, 1, 1 - own_part)
    for block in range(2, chans - 1):
        predict(0, block)
    queue = [(0, chans - 1)]
    for step in range(1, groups):
        for part in range(2):
            await_part(step, part)
        for part in range(2):
            make_table(step, part)
        for unit in queue + [(step, 0)]:
            predict(*unit)
        queue = [(1, 1)] if step == 1 else []
    done = [[], [(1, 1)]] + [[]] * chans

    for block in range(chans - 1):
        units = [(step, block + 1) for step in range(1, groups)]
        units = [unit for unit in units if unit not in done[block + 1]]
        slots = len(units) * (width // CHUNK)

        def between(turn):
            for owner in range(devices * turn // slots, devices * (turn + 1) // slots):
                prods[owner, :, 0 : 2 * TS] += product(owner, block)

        for index, unit in enumerate(units):
            base = index * (width // CHUNK)
            predict(*unit, between=lambda chunk: between(base + chunk))

    def turned(value, shift):
        return pltpu.roll(value, (32 * shift) % 128, 1) if shift % 4 else value

    def finish_products(owners):
        for owner in owners:
            prods[owner, :, 0 : 2 * TS] += product(owner, chans - 1)

    def pack(owners):
        for owner in owners:
            reals, imags = [], []
            for q in range(4):
                upper = prods[owner, 8 * q : 8 * q + 8]
                lower = prods[owner, TS + 8 * q : TS + 8 * q + 8]
                reals.append(turned(upper, q) + turned(lower, q - 1))
                imags.append(turned(lower, q) - turned(upper, q - 1))
            rs_send[owner, 0:8, :] = spread(reals)
            rs_send[owner, 8:16, :] = spread(imags)

    def send(owners):
        for owner in owners:

            @pl.when(owner != me)
            def _():
                result_copy(owner, me).start()

    def owners_of(step):
        return [step * chans + j for j in range(chans)]

    def last_step(step, carry):
        finish_products(owners_of(step + 1))
        pack(owners_of(step))
        send(owners_of(step))
        return carry

    early, late = owners_of(0)[: chans // 2], owners_of(0)[chans // 2 :]
    finish_products(early)
    pack(early)
    send(early)
    finish_products(late)
    pack(late)
    send(late)
    finish_products(owners_of(1))
    lax.fori_loop(1, planes - 1, last_step, 0)
    pack(owners_of(planes - 1))
    send(owners_of(planes - 1))

    def finish(k, carry):
        there = lax.rem(me + k, devices)
        station_copy(there, me).wait_send()
        result_copy(there, me).wait_send()
        return carry

    lax.fori_loop(1, devices, finish, 0)
    for k in range(1, chans):
        source_copy(lax.rem(rank + k, chans), rank).wait_send()

    def take(k, carry):
        there = lax.rem(me + k, devices)
        result_copy(me, there).wait_recv()
        return carry

    rs_recv[me] = rs_send[me]
    lax.fori_loop(1, devices, take, 0)

    same = tile_ref[0, me] == tile_ref[1, me]
    row = lax.broadcasted_iota(jnp.int32, (8, 128), 0)
    diagonal = row + 8 * lane_group == lax.rem(lane, 32)
    clear = jnp.logical_and(diagonal, same)
    lines = lax.rem(row, 4) == lane_group
    for c in range(chans):
        total = rs_recv[c]
        for other in range(1, planes):
            total = total + rs_recv[other * chans + c]
        for part in range(2):
            value = jnp.where(clear, 0.0, total[8 * part : 8 * part + 8])
            shifted = [turned(value, shift) for shift in range(4)]
            for q in range(4):
                piece = shifted[(4 - q) % 4]
                for other in range(1, 4):
                    piece = jnp.where(lane_group == other, shifted[(other - q) % 4], piece)
                piece = jnp.where(lines, piece, 0.0)
                for half in range(2):
                    line = jnp.sum(piece[4 * half : 4 * half + 4], 0, keepdims=True)
                    at = 128 * (2 * q + half)
                    out_ref[0, c, part : part + 1, at : at + 128] = line


def on_device(positions, flux, cluster, jones, station_uvw, channels, tile_map):
    width = positions.shape[1]
    devices = lax.axis_size("src")
    scale = 1.0 / math.sqrt(width * devices)
    chans, _, dirs, per_dev = jones.shape
    tiles = devices * per_dev // TS

    groups = devices * per_dev // ROWS
    sides = [pltpu.VMEM((tiles, width // 128, 2 * TS, 128), jnp.bfloat16)] * chans
    cluster = cluster[None]
    tile_map = tile_map.T
    smem = [pltpu.SMEM(array.shape, array.dtype) for array in (tile_map, channels)]
    inputs = (positions, flux, cluster, jones, station_uvw)
    return pl.pallas_call(
        functools.partial(kernel, devices, chans, dirs, scale),
        out_shape=pltpu.VMEM((1, chans, 2, TS * TS), jnp.float32),
        in_specs=[pl.BlockSpec(memory_space=pl.ANY)] * 7,
        out_specs=pl.BlockSpec(memory_space=pltpu.VMEM),
        scratch_shapes=smem
        + [pltpu.VMEM(array.shape, array.dtype) for array in inputs]
        + [
            pltpu.VMEM((chans, 16, 128), jnp.float32),
            pltpu.VMEM((devices, 16, 128), jnp.float32),
            pltpu.VMEM((chans, 4, width), jnp.float32),
            pltpu.VMEM((chans, 4, width), jnp.float32),
            pltpu.VMEM((groups, 2, ROWS, 128), jnp.bfloat16),
            pltpu.VMEM((chans, width // 128, 128, 128), jnp.bfloat16),
            sides,
            sides,
            pltpu.VMEM((devices, 2 * TS, 128), jnp.float32),
            pltpu.VMEM((devices, 16, 128), jnp.float32),
            pltpu.VMEM((devices, 16, 128), jnp.float32),
            pltpu.SemaphoreType.DMA((devices,)),
            pltpu.SemaphoreType.DMA((devices,)),
            pltpu.SemaphoreType.DMA((chans,)),
            pltpu.SemaphoreType.DMA((chans,)),
            pltpu.SemaphoreType.DMA((devices,)),
            pltpu.SemaphoreType.DMA((devices,)),
            pltpu.SemaphoreType.DMA((7,)),
            pltpu.SemaphoreType.REGULAR((devices // chans,)),
        ],
        compiler_params=pltpu.CompilerParams(collective_id=0, has_side_effects=True),
    )(tile_map, channels, *inputs)


def solution(mesh):
    in_specs = (
        P(None, ("group", "src")),
        P(None, ("group", "src")),
        P(("group", "src")),
        P(None, None, None, ("group", "src")),
        P(None, ("group", "src")),
        P("group"),
        P("group", None),
    )
    out_specs = P(("group", "src"), None, None, None)
    return jax.shard_map(
        on_device, mesh=mesh, in_specs=in_specs, out_specs=out_specs, check_vma=False
    )
```

```python
import functools
import math

import jax
import jax.numpy as jnp
from jax import lax
from jax.experimental import pallas as pl
from jax.experimental.pallas import tpu as pltpu
from jax.sharding import PartitionSpec as P

MESH = pl.DeviceIdType.MESH
TS = 32
ROWS = 128
CHUNK = 256
SINE = (3.1415820121765137, -5.167142868041992, 2.5418992042541504, -0.5546366572380066)
LEAD = SINE[-1]
MONIC = tuple(coef / LEAD for coef in SINE[:-1])
ATAN = (
    0.15915492177009583,
    -0.05305047705769539,
    0.031808558851480484,
    -0.022538291290402412,
    0.016709571704268456,
    -0.011514591053128242,
    0.006331328768283129,
    -0.0022920165210962296,
    0.00039099203422665596,
)
ONE = (1.0 + 6e-7) / (LEAD * LEAD)
HALF = 0.5 / (LEAD * LEAD)


def horner(coefs, y):
    total = jnp.float32(coefs[-1])
    for coef in coefs[-2::-1]:
        total = total * y + jnp.float32(coef)
    return total


def three_parts(value):
    first = value.astype(jnp.bfloat16).astype(jnp.float32)
    rest = value - first
    second = rest.astype(jnp.bfloat16).astype(jnp.float32)
    return first, second, rest - second


def polar(real, imag):
    wide, tall = jnp.abs(real), jnp.abs(imag)
    large, small = jnp.maximum(wide, tall), jnp.minimum(wide, tall)
    ratio = small / jnp.where(large > 0.0, large, 1.0)
    square = ratio * ratio
    size = large * jnp.sqrt(1.0 + square)
    angle = ratio * horner(ATAN, square)
    angle = jnp.where(tall > wide, 0.25 - angle, angle)
    angle = jnp.where(real < 0.0, 0.5 - angle, angle)
    return size, jnp.where(imag < 0.0, -angle, angle)


def nearest_first(own, step, count):
    spare = count - 1 - own
    reach = jnp.minimum(own, spare)
    half = (step + 1) // 2
    near = own + jnp.where(lax.rem(step, 2) == 1, -half, half)
    return jnp.where(step <= 2 * reach, near, jnp.where(own < spare, step, count - 1 - step))


def kernel(
    devices,
    chans,
    dirs,
    scale,
    tile_in,
    channel_in,
    position_in,
    flux_in,
    cluster_in,
    jones_in,
    uvw_in,
    out_ref,
    tile_ref,
    channel_ref,
    position_ref,
    flux_ref,
    cluster_ref,
    jones_ref,
    uvw_ref,
    st_send,
    st_recv,
    so_send,
    so_recv,
    table,
    feats,
    plain,
    weighted,
    prods,
    rs_send,
    rs_recv,
    st_sent,
    st_came,
    so_sent,
    so_came,
    rs_sent,
    rs_came,
    loaded,
    ready,
):
    me = lax.axis_index("src")
    rank = lax.rem(me, chans)
    planes = devices // chans
    plane = me // chans
    width = position_ref.shape[1]
    per_dev = uvw_ref.shape[1]
    parts = per_dev // 8
    per_group = ROWS // per_dev
    part_devices = per_group // 2
    groups = devices // per_group
    group = me // per_group

    def slot_of(block):
        outer = lax.rem(rank // 2 + block // 2, chans // 2)
        return 2 * outer + lax.rem(rank + block, 2)

    barrier = pltpu.get_barrier_semaphore()

    loads = [
        pltpu.make_async_copy(source, target, loaded.at[index])
        for index, (source, target) in enumerate(
            (
                (jones_in, jones_ref),
                (uvw_in, uvw_ref),
                (channel_in, channel_ref),
                (position_in, position_ref),
                (flux_in, flux_ref),
                (cluster_in, cluster_ref),
                (tile_in, tile_ref),
            )
        )
    ]
    for load in loads:
        load.start()

    def greet(there, carry):
        @pl.when(there != me)
        def _():
            pl.semaphore_signal(barrier, inc=1, device_id={"src": there}, device_id_type=MESH)

        return carry

    lax.fori_loop(plane * chans, devices, greet, 0)
    pl.semaphore_wait(barrier, plane * chans + chans - 1)

    def answer(there, carry):
        pl.semaphore_signal(
            ready.at[plane], inc=1, device_id={"src": there}, device_id_type=MESH
        )
        return carry

    lax.fori_loop(0, plane * chans, answer, 0)

    for load in loads:
        load.wait()

    lane = lax.broadcasted_iota(jnp.int32, (8, 128), 1)
    lane_group = lane // 32
    eight = lax.broadcasted_iota(jnp.int32, (8, per_dev), 0)
    coords = jnp.where(eight == 0, uvw_ref[0:1, :], 0.0)
    coords = jnp.where(eight == 1, uvw_ref[1:2, :], coords)
    coords = jnp.where(eight == 2, uvw_ref[2:3, :], coords)
    coords = jnp.concatenate([coords] * 16, 0).T
    features = []
    for c in range(chans):
        size, angle = polar(jones_ref[c, 0], jones_ref[c, 1])
        features += [-angle, (2.0 * LEAD * LEAD) * size]
    features = jnp.concatenate(features, 0).T

    def spread(pieces):
        total = pieces[0]
        for index, piece in enumerate(pieces[1:], 1):
            total = jnp.where(lane_group == index, piece, total)
        return total

    own_coords = spread([coords[8 * q : 8 * q + 8] for q in range(parts)])
    for c in range(chans):
        freq_ratio = 1.0 + 0.002 * channel_ref[c].astype(jnp.float32)
        pieces = [features[8 * q : 8 * q + 8] for q in range(parts)]
        pieces = [
            pltpu.roll(piece, (32 * (q - c)) % 128, 1) if q != c else piece
            for q, piece in enumerate(pieces)
        ]
        st_send[c, 0:8, :] = spread(pieces)
        st_send[c, 8:16, :] = own_coords * freq_ratio
    clusters = cluster_ref[...].astype(jnp.float32)
    for c in range(chans):
        so_send[c, 0:2, :] = position_ref[...]
        so_send[c, 2:3, :] = clusters
        so_send[c, 3:4, :] = flux_ref[c : c + 1, :]
    st_recv[me] = st_send[rank]
    so_recv[rank] = so_send[rank]

    def source_copy(there_rank, slot):
        return pltpu.make_async_remote_copy(
            src_ref=so_send.at[there_rank],
            dst_ref=so_recv.at[slot],
            send_sem=so_sent.at[0],
            recv_sem=so_came.at[slot],
            device_id={"src": plane * chans + there_rank},
            device_id_type=MESH,
        )

    def station_copy(there, slot):
        return pltpu.make_async_remote_copy(
            src_ref=st_send.at[lax.rem(there, chans)],
            dst_ref=st_recv.at[slot],
            send_sem=st_sent.at[0],
            recv_sem=st_came.at[slot // part_devices],
            device_id={"src": there},
            device_id_type=MESH,
        )

    def result_copy(there, slot):
        return pltpu.make_async_remote_copy(
            src_ref=rs_send.at[there],
            dst_ref=rs_recv.at[slot],
            send_sem=rs_sent.at[0],
            recv_sem=rs_came.at[0],
            device_id={"src": there},
            device_id_type=MESH,
        )

    def several(buffer, count, sent, came):
        return pltpu.make_async_remote_copy(
            src_ref=buffer.at[pl.ds(0, count)],
            dst_ref=buffer.at[pl.ds(0, count)],
            send_sem=sent.at[0],
            recv_sem=came,
            device_id={"src": plane * chans + slot_of(1)},
            device_id_type=MESH,
        )

    for k in range(1, chans):
        there = slot_of(k)
        source_copy(there, rank).start()
        station_copy(plane * chans + there, me).start()

    def send_stations(there, carry):
        station_copy(there, me).start()
        return carry

    def send_above(above, carry):
        pl.semaphore_wait(ready.at[above], chans)
        return lax.fori_loop(above * chans, above * chans + chans, send_stations, carry)

    lax.fori_loop(0, plane * chans, send_stations, 0)

    eight = lax.broadcasted_iota(jnp.int32, (8, width), 0)
    kinds = lax.broadcasted_iota(jnp.int32, (dirs, width), 0).astype(jnp.float32)

    def make_features(block, slot):
        l_row, m_row = so_recv[slot, 0:1, :], so_recv[slot, 1:2, :]
        n_row = jnp.sqrt(1.0 - l_row * l_row - m_row * m_row) - 1.0
        rows = jnp.where(eight == 0, l_row, jnp.where(eight == 1, m_row, 0.0))
        rows = jnp.where(eight == 2, n_row, rows)
        first, second, third = three_parts(rows)
        onehot = jnp.where(kinds == so_recv[slot, 2:3, :], 1.0, 0.0).astype(jnp.bfloat16)
        pieces = [(16 * index, onehot) for index in range(4)]
        pairs = ((first, second), (third, first), (second, first), (third, second))
        for index, pair in enumerate(pairs):
            pieces.append((64 + 16 * index, jnp.concatenate(pair, 0).astype(jnp.bfloat16)))
        for at, piece in pieces:
            for lanes in range(width // 128):
                feats[block, lanes, at : at + 16, :] = piece[:, 128 * lanes : 128 * lanes + 128]

    def take_source(block):
        slot = slot_of(block)
        if block:
            source_copy(rank, slot).wait_recv()
        make_features(block, slot)

    take_source(0)
    take_source(1)

    wide_lane = lax.broadcasted_iota(jnp.int32, (16, 128), 1)
    is_size = jnp.logical_and(wide_lane < 64, lax.rem(wide_lane, 32) >= 16)
    lane_slot = lax.rem(lane, 32) // 8

    own_part = lax.rem(me, per_group) // part_devices

    def await_part(step, part, missing=0):
        index = nearest_first(group, step, groups) * 2 + part
        count = part_devices - missing
        if count:
            several(st_recv, count, st_sent, st_came.at[index]).wait_recv()

    def make_table(step, part):
        first_device = nearest_first(group, step, groups) * per_group + part * part_devices
        blocks = []
        for j in range(part_devices):
            payload = st_recv[first_device + j]
            head, tail, _ = three_parts(payload[0:8])
            first, second, third = three_parts(payload[8:16])
            left = jnp.where(lane_slot == 3, second, first)
            right = jnp.where(lax.rem(lane_slot, 2) == 0, second, third)
            for q in range(parts):
                pieces = [
                    pltpu.roll(piece, (32 * (g - q)) % 128, 1) if g != q else piece
                    for g, piece in enumerate((head, tail, left, right))
                ]
                blocks.append(spread(pieces))
        for pair in range(ROWS // 32):
            value = jnp.concatenate(blocks[2 * pair : 2 * pair + 2], 0)
            at = 16 * pair
            table[step, part, at : at + 16, :] = jnp.where(is_size, 0.0, value).astype(
                jnp.bfloat16
            )
            below = ROWS // 2 + at
            table[step, part, below : below + 16, :] = jnp.where(is_size, value, 0.0).astype(
                jnp.bfloat16
            )

    def predict(step, block, part=None, between=None):
        base = nearest_first(group, step, groups) * (ROWS // TS)
        slot = slot_of(block)
        if part is None:
            rows = jnp.concatenate([table[step, 0], table[step, 1]], 0)
        else:
            rows = table[step, part]
            base = base + part * (ROWS // TS // 2)
        for chunk in range(width // CHUNK):
            cols = slice(chunk * CHUNK, chunk * CHUNK + CHUNK)
            weight = so_recv[slot, 3:4, cols] * scale
            begin = chunk * (CHUNK // 128)
            wide = [feats[block, begin + index] for index in range(CHUNK // 128)]
            found = jnp.dot(rows, jnp.concatenate(wide, 1), preferred_element_type=jnp.float32)
            for tile in range(rows.shape[0] // (2 * TS)):
                top = tile // 2 * ROWS + tile % 2 * TS
                turns = found[top : top + TS]
                double = found[top + ROWS // 2 : top + ROWS // 2 + TS]
                turns = turns - jnp.round(turns)
                square = turns * turns
                poly = square + jnp.float32(MONIC[2])
                poly = poly * square + jnp.float32(MONIC[1])
                poly = poly * square + jnp.float32(MONIC[0])
                sine = turns * poly
                square = sine * sine
                rest = ONE - square
                cosine = rest * lax.rsqrt(rest)
                real = double * (HALF - square)
                imag = (double * sine) * cosine
                at = base + tile
                results = (
                    (plain[block], 0, real),
                    (plain[block], TS, imag),
                    (weighted[block], 0, real * weight),
                    (weighted[block], TS, imag * weight),
                )
                for side, top, value in results:
                    value = value.astype(jnp.bfloat16)
                    for index_in in range(CHUNK // 128):
                        side[at, begin + index_in, top : top + TS, :] = value[
                            :, 128 * index_in : 128 * index_in + 128
                        ]
            if between is not None:
                between(chunk)

    contract = (((1,), (1,)), ((), ()))
    prods[...] = jnp.zeros_like(prods)

    def product(owner, block):
        first, second = tile_ref[0, owner], tile_ref[1, owner]
        lanes = range(width // 128)
        left = jnp.concatenate([weighted[block][first, index] for index in lanes], 1)
        right = jnp.concatenate([plain[block][second, index] for index in lanes], 1)
        return lax.dot_general(left, right, contract, preferred_element_type=jnp.float32)

    await_part(0, own_part, 1)
    make_table(0, own_part)
    predict(0, 0, own_part)
    predict(0, 1, own_part)
    lax.fori_loop(plane + 1, planes, send_above, 0)
    await_part(0, 1 - own_part)
    make_table(0, 1 - own_part)
    for block in range(2, chans):
        take_source(block)
    predict(0, 0, 1 - own_part)
    predict(0, 1, 1 - own_part)
    for block in range(2, chans - 1):
        predict(0, block)
    queue = [(0, chans - 1)]
    for step in range(1, groups):
        for part in range(2):
            await_part(step, part)
        for part in range(2):
            make_table(step, part)
        for unit in queue + [(step, 0)]:
            predict(*unit)
        queue = [(1, 1)] if step == 1 else []
    done = [[], [(1, 1)]] + [[]] * chans

    for block in range(chans - 1):
        units = [(step, block + 1) for step in range(1, groups)]
        units = [unit for unit in units if unit not in done[block + 1]]
        slots = len(units) * (width // CHUNK)

        def between(turn):
            for owner in range(devices * turn // slots, devices * (turn + 1) // slots):
                prods[owner, :, 0 : 2 * TS] += product(owner, block)

        for index, unit in enumerate(units):
            base = index * (width // CHUNK)
            predict(*unit, between=lambda chunk: between(base + chunk))

    def turned(value, shift):
        return pltpu.roll(value, (32 * shift) % 128, 1) if shift % 4 else value

    def finish_products(owners):
        for owner in owners:
            prods[owner, :, 0 : 2 * TS] += product(owner, chans - 1)

    def pack(owners):
        for owner in owners:
            reals, imags = [], []
            for q in range(4):
                upper = prods[owner, 8 * q : 8 * q + 8]
                lower = prods[owner, TS + 8 * q : TS + 8 * q + 8]
                reals.append(turned(upper, q) + turned(lower, q - 1))
                imags.append(turned(lower, q) - turned(upper, q - 1))
            rs_send[owner, 0:8, :] = spread(reals)
            rs_send[owner, 8:16, :] = spread(imags)

    def send(owners):
        for owner in owners:

            @pl.when(owner != me)
            def _():
                result_copy(owner, me).start()

    def owners_of(step):
        return [step * chans + j for j in range(chans)]

    def last_step(step, carry):
        finish_products(owners_of(step + 1))
        pack(owners_of(step))
        send(owners_of(step))
        return carry

    early, late = owners_of(0)[: chans // 2], owners_of(0)[chans // 2 :]
    finish_products(early)
    pack(early)
    send(early)
    finish_products(late)
    pack(late)
    send(late)
    finish_products(owners_of(1))
    lax.fori_loop(1, planes - 1, last_step, 0)
    pack(owners_of(planes - 1))
    send(owners_of(planes - 1))

    several(st_recv, devices - 1, st_sent, st_came.at[0]).wait_send()
    several(so_recv, chans - 1, so_sent, so_came.at[0]).wait_send()
    several(rs_recv, devices - 1, rs_sent, rs_came.at[0]).wait_send()
    rs_recv[me] = rs_send[me]
    several(rs_recv, devices - 1, rs_sent, rs_came.at[0]).wait_recv()

    same = tile_ref[0, me] == tile_ref[1, me]
    row = lax.broadcasted_iota(jnp.int32, (8, 128), 0)
    diagonal = row + 8 * lane_group == lax.rem(lane, 32)
    clear = jnp.logical_and(diagonal, same)
    lines = lax.rem(row, 4) == lane_group
    for c in range(chans):
        total = rs_recv[c]
        for other in range(1, planes):
            total = total + rs_recv[other * chans + c]
        for part in range(2):
            value = jnp.where(clear, 0.0, total[8 * part : 8 * part + 8])
            shifted = [turned(value, shift) for shift in range(4)]
            for q in range(4):
                piece = shifted[(4 - q) % 4]
                for other in range(1, 4):
                    piece = jnp.where(lane_group == other, shifted[(other - q) % 4], piece)
                piece = jnp.where(lines, piece, 0.0)
                for half in range(2):
                    line = jnp.sum(piece[4 * half : 4 * half + 4], 0, keepdims=True)
                    at = 128 * (2 * q + half)
                    out_ref[0, c, part : part + 1, at : at + 128] = line


def on_device(positions, flux, cluster, jones, station_uvw, channels, tile_map):
    width = positions.shape[1]
    devices = lax.axis_size("src")
    scale = 1.0 / math.sqrt(width * devices)
    chans, _, dirs, per_dev = jones.shape
    tiles = devices * per_dev // TS

    groups = devices * per_dev // ROWS
    sides = [pltpu.VMEM((tiles, width // 128, 2 * TS, 128), jnp.bfloat16)] * chans
    cluster = cluster[None]
    tile_map = tile_map.T
    smem = [pltpu.SMEM(array.shape, array.dtype) for array in (tile_map, channels)]
    inputs = (positions, flux, cluster, jones, station_uvw)
    return pl.pallas_call(
        functools.partial(kernel, devices, chans, dirs, scale),
        out_shape=pltpu.VMEM((1, chans, 2, TS * TS), jnp.float32),
        in_specs=[pl.BlockSpec(memory_space=pl.ANY)] * 7,
        out_specs=pl.BlockSpec(memory_space=pltpu.VMEM),
        scratch_shapes=smem
        + [pltpu.VMEM(array.shape, array.dtype) for array in inputs]
        + [
            pltpu.VMEM((chans, 16, 128), jnp.float32),
            pltpu.VMEM((devices, 16, 128), jnp.float32),
            pltpu.VMEM((chans, 4, width), jnp.float32),
            pltpu.VMEM((chans, 4, width), jnp.float32),
            pltpu.VMEM((groups, 2, ROWS, 128), jnp.bfloat16),
            pltpu.VMEM((chans, width // 128, 128, 128), jnp.bfloat16),
            sides,
            sides,
            pltpu.VMEM((devices, 2 * TS, 128), jnp.float32),
            pltpu.VMEM((devices, 16, 128), jnp.float32),
            pltpu.VMEM((devices, 16, 128), jnp.float32),
            pltpu.SemaphoreType.DMA((1,)),
            pltpu.SemaphoreType.DMA((2 * groups,)),
            pltpu.SemaphoreType.DMA((1,)),
            pltpu.SemaphoreType.DMA((chans,)),
            pltpu.SemaphoreType.DMA((1,)),
            pltpu.SemaphoreType.DMA((1,)),
            pltpu.SemaphoreType.DMA((7,)),
            pltpu.SemaphoreType.REGULAR((devices // chans,)),
        ],
        compiler_params=pltpu.CompilerParams(collective_id=0, has_side_effects=True),
    )(tile_map, channels, *inputs)


def solution(mesh):
    in_specs = (
        P(None, ("group", "src")),
        P(None, ("group", "src")),
        P(("group", "src")),
        P(None, None, None, ("group", "src")),
        P(None, ("group", "src")),
        P("group"),
        P("group", None),
    )
    out_specs = P(("group", "src"), None, None, None)
    return jax.shard_map(
        on_device, mesh=mesh, in_specs=in_specs, out_specs=out_specs, check_vma=False
    )
```

```python
import functools
import math

import jax
import jax.numpy as jnp
from jax import lax
from jax.experimental import pallas as pl
from jax.experimental.pallas import tpu as pltpu
from jax.sharding import PartitionSpec as P

MESH = pl.DeviceIdType.MESH
TS = 32
ROWS = 128
CHUNK = 256
SINE = (3.1415820121765137, -5.167142868041992, 2.5418992042541504, -0.5546366572380066)
LEAD = SINE[-1]
MONIC = tuple(coef / LEAD for coef in SINE[:-1])
ATAN = (
    0.15915492177009583,
    -0.05305047705769539,
    0.031808558851480484,
    -0.022538291290402412,
    0.016709571704268456,
    -0.011514591053128242,
    0.006331328768283129,
    -0.0022920165210962296,
    0.00039099203422665596,
)
ONE = (1.0 + 6e-7) / (LEAD * LEAD)
HALF = 0.5 / (LEAD * LEAD)


def horner(coefs, y):
    total = jnp.float32(coefs[-1])
    for coef in coefs[-2::-1]:
        total = total * y + jnp.float32(coef)
    return total


def three_parts(value):
    first = value.astype(jnp.bfloat16).astype(jnp.float32)
    rest = value - first
    second = rest.astype(jnp.bfloat16).astype(jnp.float32)
    return first, second, rest - second


def polar(real, imag):
    wide, tall = jnp.abs(real), jnp.abs(imag)
    large, small = jnp.maximum(wide, tall), jnp.minimum(wide, tall)
    ratio = small / jnp.where(large > 0.0, large, 1.0)
    square = ratio * ratio
    size = large * jnp.sqrt(1.0 + square)
    angle = ratio * horner(ATAN, square)
    angle = jnp.where(tall > wide, 0.25 - angle, angle)
    angle = jnp.where(real < 0.0, 0.5 - angle, angle)
    return size, jnp.where(imag < 0.0, -angle, angle)


def nearest_first(own, step, count):
    spare = count - 1 - own
    reach = jnp.minimum(own, spare)
    half = (step + 1) // 2
    near = own + jnp.where(lax.rem(step, 2) == 1, -half, half)
    return jnp.where(step <= 2 * reach, near, jnp.where(own < spare, step, count - 1 - step))


def kernel(
    devices,
    chans,
    dirs,
    scale,
    tile_in,
    channel_in,
    position_in,
    flux_in,
    cluster_in,
    jones_in,
    uvw_in,
    out_ref,
    tile_ref,
    channel_ref,
    position_ref,
    flux_ref,
    cluster_ref,
    jones_ref,
    uvw_ref,
    st_send,
    st_recv,
    so_send,
    so_recv,
    table,
    feats,
    plain,
    weighted,
    prods,
    rs_send,
    rs_recv,
    st_sent,
    st_came,
    so_sent,
    so_came,
    rs_sent,
    rs_came,
    loaded,
    ready,
):
    me = lax.axis_index("src")
    rank = lax.rem(me, chans)
    planes = devices // chans
    plane = me // chans
    width = position_ref.shape[1]
    per_dev = uvw_ref.shape[1]
    parts = per_dev // 8
    per_group = ROWS // per_dev
    part_devices = per_group // 2
    groups = devices // per_group
    group = me // per_group

    def slot_of(block):
        outer = lax.rem(rank // 2 + block // 2, chans // 2)
        return 2 * outer + lax.rem(rank + block, 2)

    barrier = pltpu.get_barrier_semaphore()

    loads = [
        pltpu.make_async_copy(source, target, loaded.at[index])
        for index, (source, target) in enumerate(
            (
                (jones_in, jones_ref),
                (uvw_in, uvw_ref),
                (channel_in, channel_ref),
                (position_in, position_ref),
                (flux_in, flux_ref),
                (cluster_in, cluster_ref),
                (tile_in, tile_ref),
            )
        )
    ]
    for load in loads:
        load.start()

    def greet(there, carry):
        @pl.when(there != me)
        def _():
            pl.semaphore_signal(barrier, inc=1, device_id={"src": there}, device_id_type=MESH)

        return carry

    lax.fori_loop(plane * chans, devices, greet, 0)
    pl.semaphore_wait(barrier, plane * chans + chans - 1)

    def answer(there, carry):
        pl.semaphore_signal(
            ready.at[plane], inc=1, device_id={"src": there}, device_id_type=MESH
        )
        return carry

    lax.fori_loop(0, plane * chans, answer, 0)

    for load in loads:
        load.wait()

    lane = lax.broadcasted_iota(jnp.int32, (8, 128), 1)
    lane_group = lane // 32
    features = []
    for c in range(chans):
        size, angle = polar(jones_ref[c, 0], jones_ref[c, 1])
        features += [-angle, (2.0 * LEAD * LEAD) * size]
    features = jnp.concatenate(features, 0).T

    def spread(pieces):
        total = pieces[0]
        for index, piece in enumerate(pieces[1:], 1):
            total = jnp.where(lane_group == index, piece, total)
        return total

    for c in range(chans):
        freq_ratio = 1.0 + 0.002 * channel_ref[c].astype(jnp.float32)
        pieces = [features[8 * q : 8 * q + 8] for q in range(parts)]
        pieces = [
            pltpu.roll(piece, (32 * (q - c)) % 128, 1) if q != c else piece
            for q, piece in enumerate(pieces)
        ]
        st_send[c, 0:8, :] = spread(pieces)
        st_send[c, 8:9, :] = jnp.zeros((1, 128), jnp.float32)
        for axis in range(3):
            place = slice(32 * axis, 32 * axis + per_dev)
            st_send[c, 8:9, place] = uvw_ref[axis : axis + 1, :] * freq_ratio
    clusters = cluster_ref[...].astype(jnp.float32)
    for c in range(chans):
        so_send[c, 0:2, :] = position_ref[...]
        so_send[c, 2:3, :] = clusters
        so_send[c, 3:4, :] = flux_ref[c : c + 1, :]
    st_recv[me] = st_send[rank]
    so_recv[rank] = so_send[rank]

    def source_copy(there_rank, slot):
        return pltpu.make_async_remote_copy(
            src_ref=so_send.at[there_rank],
            dst_ref=so_recv.at[slot],
            send_sem=so_sent.at[0],
            recv_sem=so_came.at[slot],
            device_id={"src": plane * chans + there_rank},
            device_id_type=MESH,
        )

    def station_copy(there, slot):
        return pltpu.make_async_remote_copy(
            src_ref=st_send.at[lax.rem(there, chans)],
            dst_ref=st_recv.at[slot],
            send_sem=st_sent.at[0],
            recv_sem=st_came.at[slot // part_devices],
            device_id={"src": there},
            device_id_type=MESH,
        )

    def result_copy(there, slot):
        return pltpu.make_async_remote_copy(
            src_ref=rs_send.at[there],
            dst_ref=rs_recv.at[slot],
            send_sem=rs_sent.at[0],
            recv_sem=rs_came.at[0],
            device_id={"src": there},
            device_id_type=MESH,
        )

    def several(buffer, count, sent, came):
        return pltpu.make_async_remote_copy(
            src_ref=buffer.at[pl.ds(0, count)],
            dst_ref=buffer.at[pl.ds(0, count)],
            send_sem=sent.at[0],
            recv_sem=came,
            device_id={"src": plane * chans + slot_of(1)},
            device_id_type=MESH,
        )

    for k in range(1, chans):
        there = slot_of(k)
        source_copy(there, rank).start()
        station_copy(plane * chans + there, me).start()

    def send_stations(there, carry):
        station_copy(there, me).start()
        return carry

    def send_above(above, carry):
        pl.semaphore_wait(ready.at[above], chans)
        return lax.fori_loop(above * chans, above * chans + chans, send_stations, carry)

    lax.fori_loop(0, plane * chans, send_stations, 0)

    eight = lax.broadcasted_iota(jnp.int32, (8, width), 0)
    kinds = lax.broadcasted_iota(jnp.int32, (dirs, width), 0).astype(jnp.float32)

    def make_features(block, slot):
        l_row, m_row = so_recv[slot, 0:1, :], so_recv[slot, 1:2, :]
        n_row = jnp.sqrt(1.0 - l_row * l_row - m_row * m_row) - 1.0
        rows = jnp.where(eight == 0, l_row, jnp.where(eight == 1, m_row, 0.0))
        rows = jnp.where(eight == 2, n_row, rows)
        first, second, third = three_parts(rows)
        onehot = jnp.where(kinds == so_recv[slot, 2:3, :], 1.0, 0.0).astype(jnp.bfloat16)
        pieces = [(16 * index, onehot) for index in range(4)]
        pairs = ((first, second), (third, first), (second, first), (third, second))
        for index, pair in enumerate(pairs):
            pieces.append((64 + 16 * index, jnp.concatenate(pair, 0).astype(jnp.bfloat16)))
        for at, piece in pieces:
            for lanes in range(width // 128):
                feats[block, lanes, at : at + 16, :] = piece[:, 128 * lanes : 128 * lanes + 128]

    def take_source(block):
        slot = slot_of(block)
        if block:
            source_copy(rank, slot).wait_recv()
        make_features(block, slot)

    take_source(0)
    take_source(1)

    wide_lane = lax.broadcasted_iota(jnp.int32, (16, 128), 1)
    is_size = jnp.logical_and(wide_lane < 64, lax.rem(wide_lane, 32) >= 16)
    lane_slot = lax.rem(lane, 32) // 8

    own_part = lax.rem(me, per_group) // part_devices

    def await_part(step, part, missing=0):
        index = nearest_first(group, step, groups) * 2 + part
        count = part_devices - missing
        if count:
            several(st_recv, count, st_sent, st_came.at[index]).wait_recv()

    axis_row = lax.broadcasted_iota(jnp.int32, (8, 128), 0)
    from_device = lane // per_dev

    def make_table(step, part):
        first_device = nearest_first(group, step, groups) * per_group + part * part_devices
        coords = jnp.zeros((8, 128), jnp.float32)
        for j in range(part_devices):
            line = jnp.broadcast_to(st_recv[first_device + j, 8:9, :], (8, 128))
            begin = j * per_dev
            lines = [
                pltpu.roll(line, (begin - 32 * axis) % 128, 1) if begin != 32 * axis else line
                for axis in range(3)
            ]
            value = jnp.where(axis_row == 1, lines[1], jnp.where(axis_row == 2, lines[2], 0.0))
            value = jnp.where(axis_row == 0, lines[0], value)
            coords = jnp.where(from_device == j, value, coords)
        coords = jnp.concatenate([coords[:, : ROWS // 2]] * 16, 0).T
        blocks = []
        for j in range(part_devices):
            head, tail, _ = three_parts(st_recv[first_device + j, 0:8, :])
            for q in range(parts):
                at = j * per_dev + 8 * q
                first, second, third = three_parts(coords[at : at + 8])
                left = jnp.where(lane_slot == 3, second, first)
                right = jnp.where(lax.rem(lane_slot, 2) == 0, second, third)
                pieces = [
                    pltpu.roll(piece, (32 * (g - q)) % 128, 1) if g != q else piece
                    for g, piece in enumerate((head, tail))
                ]
                blocks.append(spread(pieces + [left, right]))
        for pair in range(ROWS // 32):
            value = jnp.concatenate(blocks[2 * pair : 2 * pair + 2], 0)
            at = 16 * pair
            table[step, part, at : at + 16, :] = jnp.where(is_size, 0.0, value).astype(
                jnp.bfloat16
            )
            below = ROWS // 2 + at
            table[step, part, below : below + 16, :] = jnp.where(is_size, value, 0.0).astype(
                jnp.bfloat16
            )

    def predict(step, block, part=None, between=None):
        base = nearest_first(group, step, groups) * (ROWS // TS)
        slot = slot_of(block)
        if part is None:
            rows = jnp.concatenate([table[step, 0], table[step, 1]], 0)
        else:
            rows = table[step, part]
            base = base + part * (ROWS // TS // 2)
        for chunk in range(width // CHUNK):
            cols = slice(chunk * CHUNK, chunk * CHUNK + CHUNK)
            weight = so_recv[slot, 3:4, cols] * scale
            begin = chunk * (CHUNK // 128)
            wide = [feats[block, begin + index] for index in range(CHUNK // 128)]
            found = jnp.dot(rows, jnp.concatenate(wide, 1), preferred_element_type=jnp.float32)
            for tile in range(rows.shape[0] // (2 * TS)):
                top = tile // 2 * ROWS + tile % 2 * TS
                turns = found[top : top + TS]
                double = found[top + ROWS // 2 : top + ROWS // 2 + TS]
                turns = turns - jnp.round(turns)
                square = turns * turns
                poly = square + jnp.float32(MONIC[2])
                poly = poly * square + jnp.float32(MONIC[1])
                poly = poly * square + jnp.float32(MONIC[0])
                sine = turns * poly
                square = sine * sine
                rest = ONE - square
                cosine = rest * lax.rsqrt(rest)
                real = double * (HALF - square)
                imag = (double * sine) * cosine
                at = base + tile
                results = (
                    (plain[block], 0, real),
                    (plain[block], TS, imag),
                    (weighted[block], 0, real * weight),
                    (weighted[block], TS, imag * weight),
                )
                for side, top, value in results:
                    value = value.astype(jnp.bfloat16)
                    for index_in in range(CHUNK // 128):
                        side[at, begin + index_in, top : top + TS, :] = value[
                            :, 128 * index_in : 128 * index_in + 128
                        ]
            if between is not None:
                between(chunk)

    contract = (((1,), (1,)), ((), ()))
    prods[...] = jnp.zeros_like(prods)

    def product(owner, block):
        first, second = tile_ref[0, owner], tile_ref[1, owner]
        lanes = range(width // 128)
        left = jnp.concatenate([weighted[block][first, index] for index in lanes], 1)
        right = jnp.concatenate([plain[block][second, index] for index in lanes], 1)
        return lax.dot_general(left, right, contract, preferred_element_type=jnp.float32)

    await_part(0, own_part, 1)
    make_table(0, own_part)
    predict(0, 0, own_part)
    predict(0, 1, own_part)
    lax.fori_loop(plane + 1, planes, send_above, 0)
    await_part(0, 1 - own_part)
    make_table(0, 1 - own_part)
    for block in range(2, chans):
        take_source(block)
    predict(0, 0, 1 - own_part)
    predict(0, 1, 1 - own_part)
    for block in range(2, chans):
        predict(0, block)
    before = {2: [(1, 1)], 3: []}
    beside = {2: [(1, 2)], 3: [(2, 1)]}
    early_units = [(1, 1), (1, 2), (2, 1)]
    for step in range(1, groups):
        for unit in before.get(step, []):
            predict(*unit)
        for part in range(2):
            await_part(step, part)
        for part in range(2):
            make_table(step, part)
        for unit in beside.get(step, []):
            predict(*unit)
        predict(step, 0)

    for block in range(chans - 1):
        units = [(step, block + 1) for step in range(1, groups)]
        units = [unit for unit in units if unit not in early_units]
        slots = len(units) * (width // CHUNK)

        def between(turn):
            for owner in range(devices * turn // slots, devices * (turn + 1) // slots):
                prods[owner, :, 0 : 2 * TS] += product(owner, block)

        for index, unit in enumerate(units):
            base = index * (width // CHUNK)
            predict(*unit, between=lambda chunk: between(base + chunk))

    def turned(value, shift):
        return pltpu.roll(value, (32 * shift) % 128, 1) if shift % 4 else value

    def finish_products(owners):
        for owner in owners:
            prods[owner, :, 0 : 2 * TS] += product(owner, chans - 1)

    def pack(owners):
        for owner in owners:
            reals, imags = [], []
            for q in range(4):
                upper = prods[owner, 8 * q : 8 * q + 8]
                lower = prods[owner, TS + 8 * q : TS + 8 * q + 8]
                reals.append(turned(upper, q) + turned(lower, q - 1))
                imags.append(turned(lower, q) - turned(upper, q - 1))
            rs_send[owner, 0:8, :] = spread(reals)
            rs_send[owner, 8:16, :] = spread(imags)

    def send(owners):
        for owner in owners:

            @pl.when(owner != me)
            def _():
                result_copy(owner, me).start()

    def owners_of(step):
        return [step * chans + j for j in range(chans)]

    def last_step(step, carry):
        finish_products(owners_of(step + 1))
        pack(owners_of(step))
        send(owners_of(step))
        return carry

    early, late = owners_of(0)[: chans // 2], owners_of(0)[chans // 2 :]
    finish_products(early)
    pack(early)
    send(early)
    finish_products(late)
    pack(late)
    send(late)
    finish_products(owners_of(1))
    lax.fori_loop(1, planes - 1, last_step, 0)
    pack(owners_of(planes - 1))
    send(owners_of(planes - 1))

    several(st_recv, devices - 1, st_sent, st_came.at[0]).wait_send()
    several(so_recv, chans - 1, so_sent, so_came.at[0]).wait_send()
    several(rs_recv, devices - 1, rs_sent, rs_came.at[0]).wait_send()
    rs_recv[me] = rs_send[me]
    several(rs_recv, devices - 1, rs_sent, rs_came.at[0]).wait_recv()

    same = tile_ref[0, me] == tile_ref[1, me]
    row = lax.broadcasted_iota(jnp.int32, (8, 128), 0)
    diagonal = row + 8 * lane_group == lax.rem(lane, 32)
    clear = jnp.logical_and(diagonal, same)
    lines = lax.rem(row, 4) == lane_group
    for c in range(chans):
        total = rs_recv[c]
        for other in range(1, planes):
            total = total + rs_recv[other * chans + c]
        for part in range(2):
            value = jnp.where(clear, 0.0, total[8 * part : 8 * part + 8])
            shifted = [turned(value, shift) for shift in range(4)]
            for q in range(4):
                piece = shifted[(4 - q) % 4]
                for other in range(1, 4):
                    piece = jnp.where(lane_group == other, shifted[(other - q) % 4], piece)
                piece = jnp.where(lines, piece, 0.0)
                for half in range(2):
                    line = jnp.sum(piece[4 * half : 4 * half + 4], 0, keepdims=True)
                    at = 128 * (2 * q + half)
                    out_ref[0, c, part : part + 1, at : at + 128] = line


def on_device(positions, flux, cluster, jones, station_uvw, channels, tile_map):
    width = positions.shape[1]
    devices = lax.axis_size("src")
    scale = 1.0 / math.sqrt(width * devices)
    chans, _, dirs, per_dev = jones.shape
    tiles = devices * per_dev // TS

    groups = devices * per_dev // ROWS
    sides = [pltpu.VMEM((tiles, width // 128, 2 * TS, 128), jnp.bfloat16)] * chans
    cluster = cluster[None]
    tile_map = tile_map.T
    smem = [pltpu.SMEM(array.shape, array.dtype) for array in (tile_map, channels)]
    inputs = (positions, flux, cluster, jones, station_uvw)
    return pl.pallas_call(
        functools.partial(kernel, devices, chans, dirs, scale),
        out_shape=pltpu.VMEM((1, chans, 2, TS * TS), jnp.float32),
        in_specs=[pl.BlockSpec(memory_space=pl.ANY)] * 7,
        out_specs=pl.BlockSpec(memory_space=pltpu.VMEM),
        scratch_shapes=smem
        + [pltpu.VMEM(array.shape, array.dtype) for array in inputs]
        + [
            pltpu.VMEM((chans, 9, 128), jnp.float32),
            pltpu.VMEM((devices, 9, 128), jnp.float32),
            pltpu.VMEM((chans, 4, width), jnp.float32),
            pltpu.VMEM((chans, 4, width), jnp.float32),
            pltpu.VMEM((groups, 2, ROWS, 128), jnp.bfloat16),
            pltpu.VMEM((chans, width // 128, 128, 128), jnp.bfloat16),
            sides,
            sides,
            pltpu.VMEM((devices, 2 * TS, 128), jnp.float32),
            pltpu.VMEM((devices, 16, 128), jnp.float32),
            pltpu.VMEM((devices, 16, 128), jnp.float32),
            pltpu.SemaphoreType.DMA((1,)),
            pltpu.SemaphoreType.DMA((2 * groups,)),
            pltpu.SemaphoreType.DMA((1,)),
            pltpu.SemaphoreType.DMA((chans,)),
            pltpu.SemaphoreType.DMA((1,)),
            pltpu.SemaphoreType.DMA((1,)),
            pltpu.SemaphoreType.DMA((7,)),
            pltpu.SemaphoreType.REGULAR((devices // chans,)),
        ],
        compiler_params=pltpu.CompilerParams(collective_id=0, has_side_effects=True),
    )(tile_map, channels, *inputs)


def solution(mesh):
    in_specs = (
        P(None, ("group", "src")),
        P(None, ("group", "src")),
        P(("group", "src")),
        P(None, None, None, ("group", "src")),
        P(None, ("group", "src")),
        P("group"),
        P("group", None),
    )
    out_specs = P(("group", "src"), None, None, None)
    return jax.shard_map(
        on_device, mesh=mesh, in_specs=in_specs, out_specs=out_specs, check_vma=False
    )
```

```python
import functools
import math

import jax
import jax.numpy as jnp
from jax import lax
from jax.experimental import pallas as pl
from jax.experimental.pallas import tpu as pltpu
from jax.sharding import PartitionSpec as P

MESH = pl.DeviceIdType.MESH
TS = 32
ROWS = 128
CHUNK = 256
SINE = (3.1415820121765137, -5.167142868041992, 2.5418992042541504, -0.5546366572380066)
LEAD = SINE[-1]
MONIC = tuple(coef / LEAD for coef in SINE[:-1])
ATAN = (
    0.15915492177009583,
    -0.05305047705769539,
    0.031808558851480484,
    -0.022538291290402412,
    0.016709571704268456,
    -0.011514591053128242,
    0.006331328768283129,
    -0.0022920165210962296,
    0.00039099203422665596,
)
ONE = (1.0 + 6e-7) / (LEAD * LEAD)
HALF = 0.5 / (LEAD * LEAD)


def horner(coefs, y):
    total = jnp.float32(coefs[-1])
    for coef in coefs[-2::-1]:
        total = total * y + jnp.float32(coef)
    return total


def three_parts(value):
    first = value.astype(jnp.bfloat16).astype(jnp.float32)
    rest = value - first
    second = rest.astype(jnp.bfloat16).astype(jnp.float32)
    return first, second, rest - second


def polar(real, imag):
    wide, tall = jnp.abs(real), jnp.abs(imag)
    large, small = jnp.maximum(wide, tall), jnp.minimum(wide, tall)
    ratio = small / jnp.where(large > 0.0, large, 1.0)
    square = ratio * ratio
    size = large * jnp.sqrt(1.0 + square)
    angle = ratio * horner(ATAN, square)
    angle = jnp.where(tall > wide, 0.25 - angle, angle)
    angle = jnp.where(real < 0.0, 0.5 - angle, angle)
    return size, jnp.where(imag < 0.0, -angle, angle)


def nearest_first(own, step, count):
    spare = count - 1 - own
    reach = jnp.minimum(own, spare)
    half = (step + 1) // 2
    near = own + jnp.where(lax.rem(step, 2) == 1, -half, half)
    return jnp.where(step <= 2 * reach, near, jnp.where(own < spare, step, count - 1 - step))


def kernel(
    devices,
    chans,
    dirs,
    scale,
    tile_in,
    channel_in,
    position_in,
    flux_in,
    cluster_in,
    jones_in,
    uvw_in,
    out_ref,
    tile_ref,
    channel_ref,
    position_ref,
    flux_ref,
    cluster_ref,
    jones_ref,
    uvw_ref,
    st_send,
    st_recv,
    so_send,
    so_recv,
    table,
    feats,
    plain,
    weighted,
    prods,
    rs_send,
    rs_recv,
    st_sent,
    st_came,
    so_sent,
    so_came,
    rs_sent,
    rs_came,
    loaded,
    ready,
):
    me = lax.axis_index("src")
    rank = lax.rem(me, chans)
    planes = devices // chans
    plane = me // chans
    width = position_ref.shape[1]
    per_dev = uvw_ref.shape[1]
    parts = per_dev // 8
    per_group = ROWS // per_dev
    part_devices = per_group // 2
    groups = devices // per_group
    group = me // per_group

    def slot_of(block):
        outer = lax.rem(rank // 2 + block // 2, chans // 2)
        return 2 * outer + lax.rem(rank + block, 2)

    barrier = pltpu.get_barrier_semaphore()

    loads = [
        pltpu.make_async_copy(source, target, loaded.at[index])
        for index, (source, target) in enumerate(
            (
                (jones_in, jones_ref),
                (uvw_in, uvw_ref),
                (channel_in, channel_ref),
                (position_in, position_ref),
                (flux_in, flux_ref),
                (cluster_in, cluster_ref),
                (tile_in, tile_ref),
            )
        )
    ]
    for load in loads:
        load.start()

    def greet(there, carry):
        @pl.when(there != me)
        def _():
            pl.semaphore_signal(barrier, inc=1, device_id={"src": there}, device_id_type=MESH)

        return carry

    lax.fori_loop(plane * chans, devices, greet, 0)

    for load in loads:
        load.wait()

    lane = lax.broadcasted_iota(jnp.int32, (8, 128), 1)
    lane_group = lane // 32
    features = []
    for c in range(chans):
        size, angle = polar(jones_ref[c, 0], jones_ref[c, 1])
        features += [-angle, (2.0 * LEAD * LEAD) * size]
    features = jnp.concatenate(features, 0).T

    def spread(pieces):
        total = pieces[0]
        for index, piece in enumerate(pieces[1:], 1):
            total = jnp.where(lane_group == index, piece, total)
        return total

    for c in range(chans):
        freq_ratio = 1.0 + 0.002 * channel_ref[c].astype(jnp.float32)
        pieces = [features[8 * q : 8 * q + 8] for q in range(parts)]
        pieces = [
            pltpu.roll(piece, (32 * (q - c)) % 128, 1) if q != c else piece
            for q, piece in enumerate(pieces)
        ]
        st_send[c, 0:8, :] = spread(pieces)
        st_send[c, 8:9, :] = jnp.zeros((1, 128), jnp.float32)
        for axis in range(3):
            place = slice(32 * axis, 32 * axis + per_dev)
            st_send[c, 8:9, place] = uvw_ref[axis : axis + 1, :] * freq_ratio
    clusters = cluster_ref[...].astype(jnp.float32)
    for c in range(chans):
        so_send[c, 0:2, :] = position_ref[...]
        so_send[c, 2:3, :] = clusters
        so_send[c, 3:4, :] = flux_ref[c : c + 1, :]
    st_recv[me] = st_send[rank]
    so_recv[rank] = so_send[rank]

    pl.semaphore_wait(barrier, plane * chans + chans - 1)

    def answer(there, carry):
        pl.semaphore_signal(
            ready.at[plane], inc=1, device_id={"src": there}, device_id_type=MESH
        )
        return carry

    lax.fori_loop(0, plane * chans, answer, 0)

    def source_copy(there_rank, slot):
        return pltpu.make_async_remote_copy(
            src_ref=so_send.at[there_rank],
            dst_ref=so_recv.at[slot],
            send_sem=so_sent.at[0],
            recv_sem=so_came.at[slot],
            device_id={"src": plane * chans + there_rank},
            device_id_type=MESH,
        )

    def station_copy(there, slot):
        return pltpu.make_async_remote_copy(
            src_ref=st_send.at[lax.rem(there, chans)],
            dst_ref=st_recv.at[slot],
            send_sem=st_sent.at[0],
            recv_sem=st_came.at[slot // part_devices],
            device_id={"src": there},
            device_id_type=MESH,
        )

    def result_copy(there, slot):
        return pltpu.make_async_remote_copy(
            src_ref=rs_send.at[there],
            dst_ref=rs_recv.at[slot],
            send_sem=rs_sent.at[0],
            recv_sem=rs_came.at[0],
            device_id={"src": there},
            device_id_type=MESH,
        )

    def several(buffer, count, sent, came):
        return pltpu.make_async_remote_copy(
            src_ref=buffer.at[pl.ds(0, count)],
            dst_ref=buffer.at[pl.ds(0, count)],
            send_sem=sent.at[0],
            recv_sem=came,
            device_id={"src": plane * chans + slot_of(1)},
            device_id_type=MESH,
        )

    for k in range(1, chans):
        there = slot_of(k)
        source_copy(there, rank).start()
        station_copy(plane * chans + there, me).start()

    def send_stations(there, carry):
        station_copy(there, me).start()
        return carry

    def send_above(above, carry):
        pl.semaphore_wait(ready.at[above], chans)
        return lax.fori_loop(above * chans, above * chans + chans, send_stations, carry)

    lax.fori_loop(0, plane * chans, send_stations, 0)

    eight = lax.broadcasted_iota(jnp.int32, (8, width), 0)
    kinds = lax.broadcasted_iota(jnp.int32, (dirs, width), 0).astype(jnp.float32)

    def make_features(block, slot):
        l_row, m_row = so_recv[slot, 0:1, :], so_recv[slot, 1:2, :]
        n_row = jnp.sqrt(1.0 - l_row * l_row - m_row * m_row) - 1.0
        rows = jnp.where(eight == 0, l_row, jnp.where(eight == 1, m_row, 0.0))
        rows = jnp.where(eight == 2, n_row, rows)
        first, second, third = three_parts(rows)
        onehot = jnp.where(kinds == so_recv[slot, 2:3, :], 1.0, 0.0).astype(jnp.bfloat16)
        pieces = [(16 * index, onehot) for index in range(4)]
        pairs = ((first, second), (third, first), (second, first), (third, second))
        for index, pair in enumerate(pairs):
            pieces.append((64 + 16 * index, jnp.concatenate(pair, 0).astype(jnp.bfloat16)))
        for at, piece in pieces:
            for lanes in range(width // 128):
                feats[block, lanes, at : at + 16, :] = piece[:, 128 * lanes : 128 * lanes + 128]

    def take_source(block):
        slot = slot_of(block)
        if block:
            source_copy(rank, slot).wait_recv()
        make_features(block, slot)

    take_source(0)
    take_source(1)

    wide_lane = lax.broadcasted_iota(jnp.int32, (16, 128), 1)
    is_size = jnp.logical_and(wide_lane < 64, lax.rem(wide_lane, 32) >= 16)
    lane_slot = lax.rem(lane, 32) // 8

    own_part = lax.rem(me, per_group) // part_devices

    def await_part(step, part, missing=0):
        index = nearest_first(group, step, groups) * 2 + part
        count = part_devices - missing
        if count:
            several(st_recv, count, st_sent, st_came.at[index]).wait_recv()

    axis_row = lax.broadcasted_iota(jnp.int32, (8, 128), 0)
    from_device = lane // per_dev

    def make_table(step, part):
        first_device = nearest_first(group, step, groups) * per_group + part * part_devices
        coords = jnp.zeros((8, 128), jnp.float32)
        for j in range(part_devices):
            line = jnp.broadcast_to(st_recv[first_device + j, 8:9, :], (8, 128))
            begin = j * per_dev
            lines = [
                pltpu.roll(line, (begin - 32 * axis) % 128, 1) if begin != 32 * axis else line
                for axis in range(3)
            ]
            value = jnp.where(axis_row == 1, lines[1], jnp.where(axis_row == 2, lines[2], 0.0))
            value = jnp.where(axis_row == 0, lines[0], value)
            coords = jnp.where(from_device == j, value, coords)
        coords = jnp.concatenate([coords[:, : ROWS // 2]] * 16, 0).T
        blocks = []
        for j in range(part_devices):
            head, tail, _ = three_parts(st_recv[first_device + j, 0:8, :])
            for q in range(parts):
                at = j * per_dev + 8 * q
                first, second, third = three_parts(coords[at : at + 8])
                left = jnp.where(lane_slot == 3, second, first)
                right = jnp.where(lax.rem(lane_slot, 2) == 0, second, third)
                pieces = [
                    pltpu.roll(piece, (32 * (g - q)) % 128, 1) if g != q else piece
                    for g, piece in enumerate((head, tail))
                ]
                blocks.append(spread(pieces + [left, right]))
        for pair in range(ROWS // 32):
            value = jnp.concatenate(blocks[2 * pair : 2 * pair + 2], 0)
            at = 16 * pair
            table[step, part, at : at + 16, :] = jnp.where(is_size, 0.0, value).astype(
                jnp.bfloat16
            )
            below = ROWS // 2 + at
            table[step, part, below : below + 16, :] = jnp.where(is_size, value, 0.0).astype(
                jnp.bfloat16
            )

    def predict(step, block, part=None, between=None):
        base = nearest_first(group, step, groups) * (ROWS // TS)
        slot = slot_of(block)
        if part is None:
            rows = jnp.concatenate([table[step, 0], table[step, 1]], 0)
        else:
            rows = table[step, part]
            base = base + part * (ROWS // TS // 2)
        for chunk in range(width // CHUNK):
            cols = slice(chunk * CHUNK, chunk * CHUNK + CHUNK)
            weight = so_recv[slot, 3:4, cols] * scale
            begin = chunk * (CHUNK // 128)
            wide = [feats[block, begin + index] for index in range(CHUNK // 128)]
            found = jnp.dot(rows, jnp.concatenate(wide, 1), preferred_element_type=jnp.float32)
            for tile in range(rows.shape[0] // (2 * TS)):
                top = tile // 2 * ROWS + tile % 2 * TS
                turns = found[top : top + TS]
                double = found[top + ROWS // 2 : top + ROWS // 2 + TS]
                turns = turns - jnp.round(turns)
                square = turns * turns
                poly = square + jnp.float32(MONIC[2])
                poly = poly * square + jnp.float32(MONIC[1])
                poly = poly * square + jnp.float32(MONIC[0])
                sine = turns * poly
                square = sine * sine
                rest = ONE - square
                cosine = rest * lax.rsqrt(rest)
                real = double * (HALF - square)
                imag = (double * sine) * cosine
                at = base + tile
                results = (
                    (plain[block], 0, real),
                    (plain[block], TS, imag),
                    (weighted[block], 0, real * weight),
                    (weighted[block], TS, imag * weight),
                )
                for side, top, value in results:
                    value = value.astype(jnp.bfloat16)
                    for index_in in range(CHUNK // 128):
                        side[at, begin + index_in, top : top + TS, :] = value[
                            :, 128 * index_in : 128 * index_in + 128
                        ]
            if between is not None:
                between(chunk)

    contract = (((1,), (1,)), ((), ()))
    prods[...] = jnp.zeros_like(prods)

    def product(owner, block):
        first, second = tile_ref[0, owner], tile_ref[1, owner]
        lanes = range(width // 128)
        left = jnp.concatenate([weighted[block][first, index] for index in lanes], 1)
        right = jnp.concatenate([plain[block][second, index] for index in lanes], 1)
        return lax.dot_general(left, right, contract, preferred_element_type=jnp.float32)

    await_part(0, own_part, 1)
    make_table(0, own_part)
    predict(0, 0, own_part)
    predict(0, 1, own_part)
    lax.fori_loop(plane + 1, planes, send_above, 0)
    await_part(0, 1 - own_part)
    make_table(0, 1 - own_part)
    for block in range(2, chans):
        take_source(block)
    predict(0, 0, 1 - own_part)
    predict(0, 1, 1 - own_part)
    for block in range(2, chans):
        predict(0, block)
    beside = {1: [], 2: [(1, 2)], 3: [(2, 0)]}
    after = {1: [(1, 0), (1, 1)], 2: [], 3: [(3, 0)]}
    early_units = [(1, 1), (1, 2)]
    for step in range(1, groups):
        for part in range(2):
            await_part(step, part)
        for part in range(2):
            make_table(step, part)
        for unit in beside[step] + after[step]:
            predict(*unit)

    for block in range(chans - 1):
        units = [(step, block + 1) for step in range(1, groups)]
        units = [unit for unit in units if unit not in early_units]
        slots = len(units) * (width // CHUNK)

        def between(turn):
            for owner in range(devices * turn // slots, devices * (turn + 1) // slots):
                prods[owner, :, 0 : 2 * TS] += product(owner, block)

        for index, unit in enumerate(units):
            base = index * (width // CHUNK)
            predict(*unit, between=lambda chunk: between(base + chunk))

    def turned(value, shift):
        return pltpu.roll(value, (32 * shift) % 128, 1) if shift % 4 else value

    def finish_products(owners):
        for owner in owners:
            prods[owner, :, 0 : 2 * TS] += product(owner, chans - 1)

    def pack(owners):
        for owner in owners:
            reals, imags = [], []
            for q in range(4):
                upper = prods[owner, 8 * q : 8 * q + 8]
                lower = prods[owner, TS + 8 * q : TS + 8 * q + 8]
                reals.append(turned(upper, q) + turned(lower, q - 1))
                imags.append(turned(lower, q) - turned(upper, q - 1))
            rs_send[owner, 0:8, :] = spread(reals)
            rs_send[owner, 8:16, :] = spread(imags)

    def send(owners):
        for owner in owners:

            @pl.when(owner != me)
            def _():
                result_copy(owner, me).start()

    def owners_of(step):
        return [step * chans + j for j in range(chans)]

    def last_step(step, carry):
        finish_products(owners_of(step + 1))
        pack(owners_of(step))
        send(owners_of(step))
        return carry

    early, late = owners_of(0)[: chans // 2], owners_of(0)[chans // 2 :]
    finish_products(early)
    pack(early)
    send(early)
    finish_products(late)
    pack(late)
    send(late)
    finish_products(owners_of(1))
    lax.fori_loop(1, planes - 1, last_step, 0)
    pack(owners_of(planes - 1))
    send(owners_of(planes - 1))

    several(st_recv, devices - 1, st_sent, st_came.at[0]).wait_send()
    several(so_recv, chans - 1, so_sent, so_came.at[0]).wait_send()
    several(rs_recv, devices - 1, rs_sent, rs_came.at[0]).wait_send()
    rs_recv[me] = rs_send[me]
    several(rs_recv, devices - 1, rs_sent, rs_came.at[0]).wait_recv()

    same = tile_ref[0, me] == tile_ref[1, me]
    row = lax.broadcasted_iota(jnp.int32, (8, 128), 0)
    diagonal = row + 8 * lane_group == lax.rem(lane, 32)
    clear = jnp.logical_and(diagonal, same)
    lines = lax.rem(row, 4) == lane_group
    for c in range(chans):
        total = rs_recv[c]
        for other in range(1, planes):
            total = total + rs_recv[other * chans + c]
        for part in range(2):
            value = jnp.where(clear, 0.0, total[8 * part : 8 * part + 8])
            shifted = [turned(value, shift) for shift in range(4)]
            for q in range(4):
                piece = shifted[(4 - q) % 4]
                for other in range(1, 4):
                    piece = jnp.where(lane_group == other, shifted[(other - q) % 4], piece)
                piece = jnp.where(lines, piece, 0.0)
                for half in range(2):
                    line = jnp.sum(piece[4 * half : 4 * half + 4], 0, keepdims=True)
                    at = 128 * (2 * q + half)
                    out_ref[0, c, part : part + 1, at : at + 128] = line


def on_device(positions, flux, cluster, jones, station_uvw, channels, tile_map):
    width = positions.shape[1]
    devices = lax.axis_size("src")
    scale = 1.0 / math.sqrt(width * devices)
    chans, _, dirs, per_dev = jones.shape
    tiles = devices * per_dev // TS

    groups = devices * per_dev // ROWS
    sides = [pltpu.VMEM((tiles, width // 128, 2 * TS, 128), jnp.bfloat16)] * chans
    cluster = cluster[None]
    tile_map = tile_map.T
    smem = [pltpu.SMEM(array.shape, array.dtype) for array in (tile_map, channels)]
    inputs = (positions, flux, cluster, jones, station_uvw)
    return pl.pallas_call(
        functools.partial(kernel, devices, chans, dirs, scale),
        out_shape=pltpu.VMEM((1, chans, 2, TS * TS), jnp.float32),
        in_specs=[pl.BlockSpec(memory_space=pl.ANY)] * 7,
        out_specs=pl.BlockSpec(memory_space=pltpu.VMEM),
        scratch_shapes=smem
        + [pltpu.VMEM(array.shape, array.dtype) for array in inputs]
        + [
            pltpu.VMEM((chans, 9, 128), jnp.float32),
            pltpu.VMEM((devices, 9, 128), jnp.float32),
            pltpu.VMEM((chans, 4, width), jnp.float32),
            pltpu.VMEM((chans, 4, width), jnp.float32),
            pltpu.VMEM((groups, 2, ROWS, 128), jnp.bfloat16),
            pltpu.VMEM((chans, width // 128, 128, 128), jnp.bfloat16),
            sides,
            sides,
            pltpu.VMEM((devices, 2 * TS, 128), jnp.float32),
            pltpu.VMEM((devices, 16, 128), jnp.float32),
            pltpu.VMEM((devices, 16, 128), jnp.float32),
            pltpu.SemaphoreType.DMA((1,)),
            pltpu.SemaphoreType.DMA((2 * groups,)),
            pltpu.SemaphoreType.DMA((1,)),
            pltpu.SemaphoreType.DMA((chans,)),
            pltpu.SemaphoreType.DMA((1,)),
            pltpu.SemaphoreType.DMA((1,)),
            pltpu.SemaphoreType.DMA((7,)),
            pltpu.SemaphoreType.REGULAR((devices // chans,)),
        ],
        compiler_params=pltpu.CompilerParams(collective_id=0, has_side_effects=True),
    )(tile_map, channels, *inputs)


def solution(mesh):
    in_specs = (
        P(None, ("group", "src")),
        P(None, ("group", "src")),
        P(("group", "src")),
        P(None, None, None, ("group", "src")),
        P(None, ("group", "src")),
        P("group"),
        P("group", None),
    )
    out_specs = P(("group", "src"), None, None, None)
    return jax.shard_map(
        on_device, mesh=mesh, in_specs=in_specs, out_specs=out_specs, check_vma=False
    )
```
